128 devices in a mesh: seq: 32 (over x, z, core), tp: 4 (over y).
Axes of the slice: x: 4, y: 4, z: 4, core: 2. Of those that a mesh axis runs over, the one named last changes fastest.
Arguments:
- hidden: bfloat16 [4096, 2560], P('seq'), may hold values from -6 to 6
- gain_attn: float32 [2560], replicated, may hold values from 0.5 to 1.5
- w_query: bfloat16 [2560, 2560], P(None, 'tp')
- w_key: bfloat16 [2560, 512], P(None, 'tp'), as said below
- w_value: bfloat16 [2560, 512], P(None, 'tp'), may hold values from -0.125 to 0.125
- w_out: bfloat16 [2560, 2560], P('tp'), may hold values from -0.125 to 0.125
- gain_moe: float32 [2560], replicated, may hold values from 0.5 to 1.5
- expert_ids: int32 [4096, 6], P('seq'), may hold values from 0 to 63, all different within a row; in each aligned block of 128 rows (0 to 127, 128 to 255, ...) at most 24 rows name the same one
- expert_gates: float32 [4096, 6], P('seq'), may hold values from 0.05 to 0.3
- w_gate: bfloat16 [64, 2560, 1536], P('seq', None, 'tp'), may hold values from -0.125 to 0.125
- w_up: bfloat16 [64, 2560, 1536], P('seq', None, 'tp'), may hold values from -0.125 to 0.125
- w_down: bfloat16 [64, 1536, 2560], P('seq', 'tp'), may hold values from -0.15625 to 0.15625
- seg_lengths: int32 [16], replicated, may hold values from 1 to 1024, 4096 in all
- slot_page: int32 [2048], replicated, may hold values from -1 to 255, as said below
Outputs:
- hidden_out: bfloat16 [4096, 2560], P('seq', 'tp')
- kv_cache: bfloat16 [2048, 16, 1024], P('seq', None, 'tp')
The draws below stay inside these ranges and needn't reach their ends.
Inputs may be any that keep to these rules, and one draw needn't show every extreme that they name: `expert_ids`: a row names 6 different experts; within the 128 rows of one index of seq no expert is named by more than 24 rows. `seg_lengths`: segment lengths in order, summing to 4096. `slot_page`: owner o holds slots o * 64 to o * 64 + 63 as 2 requests of 32 slots; a request lists 1 to 32 consecutive pages (after the last page comes page 0), then -1 in its remaining slots. `w_key`: key projection of fan-in scale.
All inputs are finite; a program needn't handle non-finite values.
Results may differ from the reference program's by a relative error of at most 0.015.
Values may be sent and summed in bfloat16 or wider, within the bound.
A program may use at most 192 MiB of HBM per device.

```python
import math
import jax
import jax.numpy as jnp
import numpy as np
from jax import lax

D = 2560
Q_HEADS = 20
KV_HEADS = 4
HEAD_DIM = 128
FF = 1536
TOP = 6
TOK_DEV = 128
NSEG = 16
PAGE = 16
PAGES_REQ = 32
REQ_DEV = 2
EXPERTS = 64
TOKENS = 4096
SEG_MOST = 1024
CAP = 24
SLOTS = 64
TOTAL_SLOTS = 2048
N_SEQ = 32
N_TP = 4


def projection_pair(key):
    query_seed = jax.random.fold_in(key, 11)
    key_seed = jax.random.fold_in(key, 12)
    group_size = Q_HEADS // KV_HEADS
    kv_weights = jnp.clip(jax.random.normal(key_seed, (D, KV_HEADS, 1, HEAD_DIM), jnp.float32), -6.0, 6.0) * D ** (-0.5)
    free_part = jnp.clip(jax.random.normal(query_seed, (D, KV_HEADS, group_size, HEAD_DIM), jnp.float32), -6.0, 6.0) * D ** (-0.5)
    query_weights = free_part
    return (query_weights.reshape(D, Q_HEADS * HEAD_DIM), kv_weights.reshape(D, KV_HEADS * HEAD_DIM))


def draw_w_query(key, part):
    return projection_pair(key)[0].astype(jnp.bfloat16)


def draw_w_key(key, part):
    return projection_pair(key)[1].astype(jnp.bfloat16)


def draw_slot_page(key, part):
    npages = TOKENS // PAGE
    owners = TOTAL_SLOTS // SLOTS
    start_seed = jax.random.fold_in(key, 21)
    length_seed = jax.random.fold_in(key, 22)
    first_page = jax.random.randint(start_seed, (owners, REQ_DEV), 0, npages)
    page_count = jax.random.randint(length_seed, (owners, REQ_DEV), 1, PAGES_REQ + 1)
    first_page = first_page.at[0, 0].set(npages - PAGES_REQ)
    page_count = page_count.at[0, 0].set(PAGES_REQ).at[0, 1].set(1)
    offsets = jnp.arange(PAGES_REQ, dtype=jnp.int32)
    pages = (first_page[:, :, None] + offsets[None, None, :]) % npages
    filled = jnp.where(offsets[None, None, :] < page_count[:, :, None], pages, -1)
    return filled.reshape(TOTAL_SLOTS).astype(jnp.int32)


def block_levels(own_key, extent, pieces, low, largest):
    def one(dim, blocks):
        steps = jax.random.uniform(jax.random.fold_in(jax.random.fold_in(own_key, 6), dim), (blocks,), jnp.float32, low / len(pieces), largest / len(pieces))
        return jnp.repeat(jnp.exp(steps), extent[dim] // blocks).reshape((-1,) + (1,) * (len(extent) - dim - 1))

    level = one(*pieces[0])
    for cut in pieces[1:]:
        level = level * one(*cut)
    return level


def profile(number_of, total, most, slope):
    loads = [(1 << 20) // math.isqrt(rank ** slope) + 1 for rank in range(2, number_of + 1)]
    surplus, given = total - most - (number_of - 1), [1] * (number_of - 1)
    while surplus > 0:
        movable = [i for i in range(number_of - 1) if given[i] < most]
        pool, budget = sum([loads[i] for i in movable]), surplus
        for i in movable:
            addition = min(most - given[i], max(1, budget * loads[i] // pool), surplus)
            given[i] = given[i] + addition
            surplus = surplus - addition
    return np.array([most] + given)


def uneven_parts(stream_key, number_of, total, limit, slope):
    if number_of == 2:
        one = jax.random.randint(stream_key, (), max(1, total - limit), min(limit, total - 1) + 1)
        return jnp.stack([one, total - one])
    lengths = jnp.asarray(profile(number_of, total, limit, slope), jnp.int32)
    pairs = (number_of - 1) // 2
    giver, receiver = lengths[1:1 + 2 * pairs:2], lengths[2:2 + 2 * pairs:2]
    slack = jnp.minimum(giver - 1, limit - receiver)
    moved = jax.random.randint(jax.random.fold_in(stream_key, 1), (pairs,), 0, 1 << 20) % (slack + 1)
    lengths = lengths.at[1:1 + 2 * pairs:2].set(giver - moved).at[2:2 + 2 * pairs:2].set(receiver + moved)
    return lengths[jax.random.permutation(jax.random.fold_in(stream_key, 2), number_of)]


def assign_block(key, own, number, rows, amount, top, bound, skew):
    sequence = jax.random.permutation(key, amount)
    heavy_load, usual = load_shares(amount, rows * top, bound, skew, True), load_shares(amount, rows * top, bound, skew, False)
    places = jnp.arange(amount)

    def named(lengths, offset_by):
        used = int((lengths > 0).sum())
        fixed = max(1, used // 4)
        moved = fixed + (places - fixed + offset_by * (used - fixed)) % max(1, amount - fixed)
        return jnp.zeros((amount,), jnp.int32).at[sequence[jnp.where(places < fixed, places, moved)]].set(jnp.asarray(lengths, jnp.int32))

    lengths = jnp.where(number % 4 == 0, named(heavy_load, number // 4), named(usual, number - number // 4 - 1))
    mixed = jax.random.permutation(jax.random.fold_in(own, 3), amount)
    donor, receiver = mixed[0:amount // 2 * 2:2], mixed[1:amount // 2 * 2:2]
    slack = jnp.minimum(lengths[donor] - 1, bound - lengths[receiver]) // 2
    slack = jnp.where((donor == sequence[0]) | (receiver == sequence[0]) | (lengths[receiver] == 0), 0, jnp.maximum(slack, 0))
    moved = jax.random.randint(jax.random.fold_in(own, 4), (amount // 2,), 0, 1 << 20) % (slack + 1)
    lengths = lengths.at[donor].add(-moved).at[receiver].add(moved)
    members = jnp.searchsorted(jnp.cumsum(lengths), jnp.arange(rows * top), side="right").astype(jnp.int32)
    listing = members.reshape(top, rows).T
    listing = listing[jax.random.permutation(jax.random.fold_in(own, 1), rows)]
    offset_by = jax.random.randint(jax.random.fold_in(own, 2), (rows, 1), 0, top)
    return jnp.take_along_axis(listing, (jnp.arange(top)[None, :] + offset_by) % top, axis=1)


def load_shares(amount, total, most, slope, full):
    loads = [(1 << 20) // math.isqrt(rank ** slope) + 1 for rank in range(1, amount + 1)]
    largest = most if full else min(most, max(-(-total // amount), total * loads[0] // sum(loads)))
    least = 1 if total - largest >= amount - 1 else 0
    holding, rest = [largest] + [least] * (amount - 1), total - largest - least * (amount - 1)
    while rest > 0:
        free = [i for i in range(1, amount) if holding[i] < largest] or [i for i in range(1, amount) if holding[i] < most]
        whole, budget = sum([loads[i] for i in free]), rest
        for i in free:
            addition = min(most - holding[i], max(1, budget * loads[i] // whole), rest)
            holding[i] = holding[i] + addition
            rest = rest - addition
    return np.array(holding)


def noise(stream_key, extent, deviation, limit, shards=(), kind=jnp.bfloat16):
    entries = jax.random.normal(stream_key, extent, jnp.float32) * deviation
    if len(shards) > 0:
        entries = block_levels(stream_key, extent, shards, -0.22, 0.18) * entries
    return jnp.clip(entries, min=-limit, max=limit).astype(kind)


def setup_inputs(seed: int = 0) -> dict:
    streams_of = jax.random.split(jax.random.key(seed), 15)
    hidden = noise(streams_of[0], (TOKENS, D), 1.0, 6.0, ((0, 32),))
    gain_attn = jnp.clip(1.0 + 0.1 * jax.random.normal(streams_of[1], (D,), jnp.float32), 0.5, 1.5)
    w_query = draw_w_query(jax.random.fold_in(streams_of[14], 71), 0)
    w_key = draw_w_key(jax.random.fold_in(streams_of[14], 71), 0)
    w_value = noise(streams_of[4], (D, KV_HEADS * HEAD_DIM), D ** -0.5, 0.125, ((1, 4),))
    w_out = noise(streams_of[5], (Q_HEADS * HEAD_DIM, D), (Q_HEADS * HEAD_DIM) ** -0.5, 0.125, ((0, 4),))
    gain_moe = jnp.clip(1.0 + 0.1 * jax.random.normal(streams_of[6], (D,), jnp.float32), 0.5, 1.5)
    expert_ids_keys = jax.random.split(jax.random.fold_in(streams_of[7], 1), TOKENS // TOK_DEV)
    expert_ids_turns = jax.random.permutation(jax.random.fold_in(streams_of[7], 3), TOKENS // TOK_DEV)
    expert_ids = jax.vmap(lambda own, number: assign_block(jax.random.fold_in(streams_of[7], 2), own, number, TOK_DEV, EXPERTS, TOP, CAP, 2))(expert_ids_keys, expert_ids_turns).reshape((TOKENS, TOP))
    expert_gates = jnp.clip(0.05 + 0.25 * jax.random.uniform(streams_of[8], (TOKENS, TOP), jnp.float32) ** block_levels(streams_of[8], (TOKENS, TOP), ((0, 32),), -0.2, 0.2), 0.05, 0.3)
    w_gate = noise(streams_of[9], (EXPERTS, D, FF), D ** -0.5, 0.125, ((0, 32), (2, 4)))
    w_up = noise(streams_of[10], (EXPERTS, D, FF), D ** -0.5, 0.125, ((0, 32), (2, 4)))
    w_down = noise(streams_of[11], (EXPERTS, FF, D), FF ** -0.5, 0.15625, ((0, 32), (1, 4)))
    seg_lengths = uneven_parts(streams_of[12], NSEG, TOKENS, SEG_MOST, 2).astype(jnp.int32)
    slot_page = draw_slot_page(jax.random.fold_in(streams_of[14], 71), 0)
    return dict(hidden=hidden, gain_attn=gain_attn, w_query=w_query, w_key=w_key, w_value=w_value, w_out=w_out, gain_moe=gain_moe, expert_ids=expert_ids, expert_gates=expert_gates, w_gate=w_gate, w_up=w_up, w_down=w_down, seg_lengths=seg_lengths, slot_page=slot_page)


epsilon = 1e-05
rope_base = 500000.0
masked_score = -1e+30

def rms_norm(values, gain_vec):
    widened = values.astype(jnp.float32)
    factor = lax.rsqrt(lax.optimization_barrier(jnp.mean(widened * widened, axis=-1, keepdims=True)) + epsilon)
    return (widened * factor * gain_vec).astype(jnp.bfloat16)

def rotate(values, position):
    half_dim = values.shape[-1] // 2
    inverse = rope_base ** (-2.0 * jnp.arange(half_dim, dtype=jnp.float32) / values.shape[-1])
    angles = position.astype(jnp.float32)[:, None] * inverse[None, :]
    cosine = jnp.cos(angles)[:, None, :]
    sine_part = jnp.sin(angles)[:, None, :]
    first_half = values[..., :half_dim]
    second_half = values[..., half_dim:]
    return jnp.concatenate([first_half * cosine - second_half * sine_part, second_half * cosine + first_half * sine_part], axis=-1)

def segment_start(seg_lengths, positions):
    bounds = jnp.cumsum(seg_lengths).astype(jnp.int32)
    starts = bounds - seg_lengths.astype(jnp.int32)
    return lax.optimization_barrier(jnp.max(jnp.where(starts[None, :] <= positions[:, None], starts[None, :], 0), axis=1)).astype(jnp.int32)

def reference(hidden, gain_attn, w_query, w_key, w_value, w_out, gain_moe, expert_ids, expert_gates, w_gate, w_up, w_down, seg_lengths, slot_page):
    positions = jnp.arange(TOKENS, dtype=jnp.int32)
    seg_first = segment_start(seg_lengths, positions)
    offsets = positions - seg_first
    normed = rms_norm(hidden, gain_attn)
    group_size = Q_HEADS // KV_HEADS
    query_raw = jnp.dot(normed, w_query, preferred_element_type=jnp.float32).reshape(TOKENS, Q_HEADS, HEAD_DIM)
    queries = rotate(query_raw, offsets).astype(jnp.bfloat16)
    key_raw = jnp.dot(normed, w_key, preferred_element_type=jnp.float32).reshape(TOKENS, KV_HEADS, HEAD_DIM)
    keys_rot = rotate(key_raw, offsets).astype(jnp.bfloat16)
    values = jnp.dot(normed, w_value, preferred_element_type=jnp.float32).astype(jnp.bfloat16).reshape(TOKENS, KV_HEADS, HEAD_DIM)
    keys_wide = keys_rot.astype(jnp.float32)
    values_wide = values.astype(jnp.float32)
    block_rows = math.gcd(TOKENS, 512)
    blocks = TOKENS // block_rows
    query_blocks = queries.reshape(blocks, block_rows, KV_HEADS, group_size, HEAD_DIM)
    position_blocks = positions.reshape(blocks, block_rows)
    first_blocks = seg_first.reshape(blocks, block_rows)

    def attend(operands):
        block_query, block_pos, block_first = operands
        scores = jnp.einsum('qkgd,skd->qkgs', block_query.astype(jnp.float32), keys_wide) * HEAD_DIM ** (-0.5)
        allowed = (positions[None, :] <= block_pos[:, None]) & (positions[None, :] >= block_first[:, None])
        allowed = allowed[:, None, None, :]
        scores = jnp.where(allowed, scores, masked_score)
        row_max = lax.optimization_barrier(jnp.max(scores, axis=-1, keepdims=True))
        weights = jnp.where(allowed, jnp.exp(scores - row_max), 0.0)
        row_total = lax.optimization_barrier(jnp.sum(weights, axis=-1, keepdims=True))
        rounded = lax.optimization_barrier(weights.astype(jnp.bfloat16)).astype(jnp.float32)
        mixed_rows = jnp.einsum('qkgs,skd->qkgd', rounded, values_wide) / row_total
        return mixed_rows.astype(jnp.bfloat16)
    attended = lax.map(attend, (query_blocks, position_blocks, first_blocks)).reshape(TOKENS, Q_HEADS * HEAD_DIM)
    group_width = Q_HEADS * HEAD_DIM // N_TP
    attn_proj = jnp.zeros((TOKENS, D), jnp.float32)
    for part_index in range(N_TP):
        part_term = jnp.dot(attended[:, part_index * group_width:(part_index + 1) * group_width], w_out[part_index * group_width:(part_index + 1) * group_width], preferred_element_type=jnp.float32)
        attn_proj = attn_proj + lax.optimization_barrier(part_term.astype(jnp.bfloat16)).astype(jnp.float32)
    mid = (hidden.astype(jnp.float32) + attn_proj).astype(jnp.bfloat16)
    moe_in = rms_norm(mid, gain_moe)
    flat_ids = expert_ids.reshape(N_SEQ, TOK_DEV * TOP)
    expert_hits = (flat_ids[:, :, None] == jnp.arange(EXPERTS, dtype=jnp.int32)[None, None, :]).astype(jnp.int32)
    slot_rank = lax.optimization_barrier(jnp.sum((jnp.cumsum(expert_hits, axis=1).astype(jnp.int32) - 1) * expert_hits, axis=2)).astype(jnp.int32)
    source = jnp.arange(N_SEQ, dtype=jnp.int32)[:, None]
    slot_row = (source * CAP + slot_rank).reshape(TOKENS * TOP)
    owner_ids = flat_ids.reshape(TOKENS * TOP)
    buffer = jnp.zeros((EXPERTS, N_SEQ * CAP, D), jnp.bfloat16).at[owner_ids, slot_row].set(jnp.repeat(moe_in, TOP, axis=0))
    ff_width = FF // N_TP

    def expert(operands):
        rows_in, gate_mat, up_mat, down_mat = operands
        gate_term = jnp.dot(rows_in, gate_mat, preferred_element_type=jnp.float32)
        up_term = jnp.dot(rows_in, up_mat, preferred_element_type=jnp.float32)
        hidden_act = (jax.nn.silu(gate_term) * up_term).astype(jnp.bfloat16)
        summed = jnp.zeros((rows_in.shape[0], D), jnp.float32)
        for part_index in range(N_TP):
            part_term = jnp.dot(hidden_act[:, part_index * ff_width:(part_index + 1) * ff_width], down_mat[part_index * ff_width:(part_index + 1) * ff_width], preferred_element_type=jnp.float32)
            summed = summed + lax.optimization_barrier(part_term.astype(jnp.bfloat16)).astype(jnp.float32)
        return summed.astype(jnp.bfloat16)
    outputs = lax.map(expert, (buffer, w_gate, w_up, w_down))
    picked = outputs[owner_ids, slot_row].astype(jnp.float32).reshape(TOKENS, TOP, D)
    moe_out = jnp.einsum('tk,tkd->td', expert_gates.astype(jnp.float32), picked)
    hidden_out = (mid.astype(jnp.float32) + moe_out).astype(jnp.bfloat16)
    page_rows = jnp.stack([keys_rot, values], axis=2).reshape(TOKENS // PAGE, PAGE, KV_HEADS * 2 * HEAD_DIM)
    safe_page = jnp.maximum(slot_page, 0).astype(jnp.int32)
    kv_cache = jnp.where((slot_page >= 0)[:, None, None], page_rows[safe_page], jnp.zeros((), jnp.bfloat16))
    return (hidden_out, kv_cache)
```

```python
import functools

import jax
import jax.numpy as jnp
from jax import lax
from jax.experimental import pallas as pl
from jax.experimental.pallas import tpu as pltpu
from jax.sharding import PartitionSpec as P

HEAD_DIM = 128
TOP = 6
PAGE = 16
CAP = 24
RING = 4
MESH = pl.DeviceIdType.MESH
ANY = pl.BlockSpec(memory_space=pl.ANY)
WHOLE = pl.BlockSpec(memory_space=pltpu.VMEM)
epsilon = 1e-05
rope_base = 500000.0
masked_score = -1e30
bf16 = jnp.bfloat16
f32 = jnp.float32


def my_place():
    index = lax.axis_index("seq")
    return {
        "x": index // 8,
        "z": lax.rem(index // 2, RING),
        "c": lax.rem(index, 2),
        "y": lax.axis_index("tp"),
    }


def device_at(place):
    return ((place["x"] * RING + place["z"]) * 2 + place["c"], place["y"])


def moved(place, axis, step):
    size = 2 if axis == "c" else RING
    other = dict(place)
    other[axis] = lax.rem(place[axis] + step + size, size)
    return other


def enter(places):
    barrier = pltpu.get_barrier_semaphore()
    for place in places:
        pl.semaphore_signal(barrier, inc=1, device_id=device_at(place), device_id_type=MESH)
    pl.semaphore_wait(barrier, len(places))


class Links:
    def __init__(self, send_sem, recv_sem):
        self.send_sem, self.recv_sem, self.count = send_sem, recv_sem, 0
        self.started = []

    def push(self, src, dst, place):
        copy = pltpu.make_async_remote_copy(
            src_ref=src,
            dst_ref=dst,
            send_sem=self.send_sem.at[self.count],
            recv_sem=self.recv_sem.at[self.count],
            device_id=device_at(place),
            device_id_type=MESH,
        )
        self.count += 1
        copy.start()
        self.started.append(copy)
        return copy

    def finish(self):
        for copy in self.started:
            copy.wait_send()


def torus_gather(me, dims, parts, src, out, links, local_sem):
    sibling = moved(me, "c", 1)

    def at(where, row0, rows):
        return out.at[tuple(where[d] for d in dims) + (pl.ds(row0, rows), slice(None))]

    own = {d: me[d] for d in dims}
    local = pltpu.make_async_copy(src, at(own, 0, src.shape[0]), local_sem)
    local.start()
    to_sibling = [links.push(src, at(own, 0, src.shape[0]), sibling)]
    for phase in range(len(parts[0][3])):
        if phase == 1:
            local.wait()
        live = []
        for row0, rows, half, order in parts:
            axis = order[phase]
            base = dict(own)
            for done in order[:phase]:
                base[done] = slice(None)
            whole = at(base, row0, rows)
            source = src.at[pl.ds(row0, rows), :] if phase == 0 else whole
            up = links.push(source, whole, moved(me, axis, 1))
            down = links.push(source, whole, moved(me, axis, -1))
            live.append((row0, rows, half, order, axis, base, up, down))
        forwarded = []
        for row0, rows, half, order, axis, base, up, down in live:
            for copy, step in ((up, 1), (down, -1)):
                copy.wait_recv()
                got = dict(base)
                got[axis] = moved(me, axis, -step)[axis]
                if phase == 0:
                    r0, rn = (row0, half) if step == 1 else (row0 + half, rows - half)
                    piece = at(got, r0, rn)
                else:
                    cut = dict(got)
                    cut[order[0]] = pl.ds(0, 2) if step == 1 else pl.ds(2, 2)
                    piece = at(cut, row0, rows)
                forwarded.append(links.push(piece, piece, moved(me, axis, step)))
                there = at(got, row0, rows)
                to_sibling.append(links.push(there, there, sibling))
        for n, (row0, rows, half, order, axis, base, up, down) in enumerate(live):
            forwarded[2 * n].wait_recv()
            forwarded[2 * n + 1].wait_recv()
            got = dict(base)
            got[axis] = moved(me, axis, 2)[axis]
            there = at(got, row0, rows)
            to_sibling.append(links.push(there, there, sibling))
    for copy in to_sibling:
        copy.wait_recv()


def copies_of_gather(parts):
    phases = len(parts[0][3])
    return 1 + phases * len(parts) * 7


KV_PARTS = ((0, 80, 48, ("x", "z")), (80, 64, 32, ("z", "x")))
ROW_PARTS = (
    (0, 48, 32, ("z", "y", "x")),
    (48, 48, 32, ("y", "x", "z")),
    (96, 32, 16, ("x", "z", "y")),
)


def kv_gather_kernel(src, out, send_sem, recv_sem, local_sem):
    me = my_place()
    enter([moved(me, a, s) for a in ("x", "z") for s in (1, -1)] + [moved(me, "c", 1)])
    links = Links(send_sem, recv_sem)
    torus_gather(me, ("x", "z", "c"), KV_PARTS, src, out, links, local_sem)
    links.finish()


def kv_gather(rows):
    n = copies_of_gather(KV_PARTS)
    return pl.pallas_call(
        kv_gather_kernel,
        out_shape=jax.ShapeDtypeStruct((RING, RING, 2) + rows.shape, bf16),
        in_specs=[ANY],
        out_specs=ANY,
        scratch_shapes=[
            pltpu.SemaphoreType.DMA((n,)),
            pltpu.SemaphoreType.DMA((n,)),
            pltpu.SemaphoreType.DMA,
        ],
        compiler_params=pltpu.CompilerParams(collective_id=1, has_side_effects=True),
        name="kv_gather",
    )(rows)


def row_gather_kernel(
    terms, hidden, gain, out, mid, heard, squares, mid_v, row_v, send_sem, recv_sem, local_sem
):
    me = my_place()
    peers = [moved(me, "y", s) for s in (1, 2, 3)]
    enter(
        [moved(me, a, s) for a in ("x", "z") for s in (1, -1)] + [moved(me, "c", 1)] + peers
    )
    links = Links(send_sem, recv_sem)
    sent = [
        links.push(terms.at[peer["y"]], heard.at[n], peer) for n, peer in enumerate(peers)
    ]
    total = terms[me["y"]].astype(f32)
    for n in range(3):
        sent[n].wait_recv()
        total = total + heard[n].astype(f32)
    mid_now = (hidden[...].astype(f32) + total).astype(bf16)
    mid_v[...] = mid_now
    wide = mid_now.astype(f32)
    ours = jnp.sum(wide * wide, axis=1, keepdims=True)
    squares[3] = jnp.broadcast_to(ours, (ours.shape[0], 128))
    told = [links.push(squares.at[3], squares.at[n], peer) for n, peer in enumerate(peers)]
    whole = ours
    for n in range(3):
        told[n].wait_recv()
        whole = whole + squares[n][:, :1]
    factor = lax.rsqrt(whole * (1.0 / (RING * wide.shape[1])) + epsilon)
    row_v[...] = (wide * factor * gain[...]).astype(bf16)
    keep = pltpu.make_async_copy(mid_v, mid, local_sem.at[1])
    keep.start()
    torus_gather(me, ("x", "z", "c", "y"), ROW_PARTS, row_v, out, links, local_sem.at[0])
    keep.wait()
    links.finish()


def row_gather(terms, hidden, gain):
    n = 6 + copies_of_gather(ROW_PARTS)
    rows, cols = hidden.shape
    return pl.pallas_call(
        row_gather_kernel,
        out_shape=(
            jax.ShapeDtypeStruct((RING, RING, 2, RING, rows, cols), bf16),
            jax.ShapeDtypeStruct((rows, cols), bf16),
        ),
        in_specs=[WHOLE, WHOLE, WHOLE],
        out_specs=(ANY, ANY),
        scratch_shapes=[
            pltpu.VMEM((3, rows, cols), bf16),
            pltpu.VMEM((4, rows, 128), f32),
            pltpu.VMEM((rows, cols), bf16),
            pltpu.VMEM((rows, cols), bf16),
            pltpu.SemaphoreType.DMA((n,)),
            pltpu.SemaphoreType.DMA((n,)),
            pltpu.SemaphoreType.DMA((2,)),
        ],
        compiler_params=pltpu.CompilerParams(
            collective_id=2, has_side_effects=True, vmem_limit_bytes=16 << 20
        ),
        name="row_gather",
    )(terms, hidden, gain)


SUM_ORDERS = (("x", "y", "z"), ("z", "x", "y"), ("y", "z", "x"))
SUM_DIMS = ("x", "z", "y")


def row_sum_kernel(terms, mid, out, total, other, bufs, out_v, send_sem, recv_sem, local_sem):
    me = my_place()
    sibling = moved(me, "c", 1)
    enter([moved(me, a, s) for a in ("x", "z", "y") for s in (1, -1)] + [sibling])
    links = Links(send_sem, recv_sem)
    spans = [(row0, rows, half) for row0, rows, half, _ in ROW_PARTS]
    cols = out.shape[1]

    def held(ref, where, row0, rows):
        return ref.at[tuple(where[d] for d in SUM_DIMS) + (pl.ds(row0, rows), slice(None))]

    def add(where, row0, rows, buf):
        open_dims = [d for d in SUM_DIMS if isinstance(where[d], tuple)]
        sizes = [where[d][1] for d in open_dims]
        count = 1
        for size in sizes:
            count *= size

        def one(step, carry):
            rest, picks = step, []
            for size in reversed(sizes):
                picks.append(lax.rem(rest, size))
                rest = rest // size
            picks = picks[::-1]
            place = dict(where)
            for d, pick in zip(open_dims, picks):
                place[d] = where[d][0] + pick
            index = tuple(place[d] for d in SUM_DIMS) + (pl.ds(row0, rows), slice(None))
            total[index] = (total[index].astype(f32) + buf[tuple(picks)].astype(f32)).astype(bf16)
            return carry

        lax.fori_loop(0, count, one, 0)

    full = (0, RING)

    def sliced(where):
        return {d: pl.ds(*v) if isinstance(v, tuple) else v for d, v in where.items()}

    first = []
    slots = 0
    for step in (2, 1, 3, 0):
        for (row0, rows, half), order in zip(spans, SUM_ORDERS):
            where = {d: full for d in SUM_DIMS}
            where[order[0]] = moved(me, order[0], step)[order[0]]
            cut = sliced(where)
            mine = (cut["x"], cut["z"], me["c"], cut["y"], pl.ds(row0, rows), slice(None))
            theirs = (cut["x"], cut["z"], sibling["c"], cut["y"], pl.ds(row0, rows), slice(None))
            keep = pltpu.make_async_copy(
                terms.at[mine], held(total, cut, row0, rows), local_sem.at[slots]
            )
            keep.start()
            slots += 1
            push = links.push(terms.at[theirs], held(other, cut, row0, rows), sibling)
            first.append((where, row0, rows, keep, push))

    def settle(step, part):
        where, row0, rows, keep, push = first[(2, 1, 3, 0).index(step) * 3 + part]
        keep.wait()
        push.wait_recv()
        open_dims = [d for d in SUM_DIMS if isinstance(where[d], tuple)]

        def one(n, carry):
            place = dict(where)
            place[open_dims[0]] = n // RING
            place[open_dims[1]] = lax.rem(n, RING)
            index = tuple(place[d] for d in SUM_DIMS) + (pl.ds(row0, rows), slice(None))
            total[index] = (total[index].astype(f32) + other[index].astype(f32)).astype(bf16)
            return carry

        lax.fori_loop(0, RING * RING, one, 0)

    for phase in range(3):
        live = []
        for part, ((row0, rows, half), order) in enumerate(zip(spans, SUM_ORDERS)):
            axis = order[phase]
            base = {d: me[d] for d in SUM_DIMS}
            for later in order[phase + 1 :]:
                base[later] = full
            far, up, down = (moved(me, axis, s)[axis] for s in (2, 1, -1))
            buf_a, buf_b, buf_p, buf_m = bufs[(phase * 3 + part) * 4 : (phase * 3 + part) * 4 + 4]
            if phase == 0:
                settle(2, part)

            def half_of(index, which, base=base, axis=axis, order=order, row0=row0, rows=rows, half=half, phase=phase):
                where = dict(base)
                where[axis] = index
                if phase == 2:
                    r0, rn = (row0, half) if which == 0 else (row0 + half, rows - half)
                    return where, r0, rn
                where[order[phase + 1]] = (0, 2) if which == 0 else (2, 2)
                return where, row0, rows

            whole_of = lambda index, base=base, axis=axis: {**base, axis: index}
            where, r0, rn = half_of(far, 0)
            send_a = links.push(held(total, sliced(where), r0, rn), buf_a, moved(me, axis, 1))
            where, r0, rn = half_of(far, 1)
            send_b = links.push(held(total, sliced(where), r0, rn), buf_b, moved(me, axis, -1))
            live.append((row0, rows, axis, up, down, half_of, whole_of, send_a, send_b, buf_a, buf_b, buf_p, buf_m))
        second = []
        for part, (row0, rows, axis, up, down, half_of, whole_of, send_a, send_b, buf_a, buf_b, buf_p, buf_m) in enumerate(live):
            if phase == 0:
                settle(1, part)
            send_a.wait_recv()
            add(*half_of(up, 0), buf_a)
            push_p = links.push(held(total, sliced(whole_of(up)), row0, rows), buf_p, moved(me, axis, 1))
            if phase == 0:
                settle(3, part)
            send_b.wait_recv()
            add(*half_of(down, 1), buf_b)
            push_m = links.push(held(total, sliced(whole_of(down)), row0, rows), buf_m, moved(me, axis, -1))
            second.append((push_p, push_m))
        for part, (row0, rows, axis, up, down, half_of, whole_of, send_a, send_b, buf_a, buf_b, buf_p, buf_m) in enumerate(live):
            if phase == 0:
                settle(0, part)
            push_p, push_m = second[part]
            push_p.wait_recv()
            add(whole_of(me[axis]), row0, rows, buf_p)
            push_m.wait_recv()
            add(whole_of(me[axis]), row0, rows, buf_m)
    out_v[...] = (mid[...].astype(f32) + total[me["x"], me["z"], me["y"]].astype(f32)).astype(bf16)
    done = pltpu.make_async_copy(out_v, out, local_sem.at[slots])
    done.start()
    done.wait()
    links.finish()


def row_sum(terms, mid):
    rows, cols = mid.shape
    n = 12 + 36
    bufs = []
    for phase in range(3):
        for (_, part_rows, half, _), order in zip(ROW_PARTS, SUM_ORDERS):
            open_dims = [d for d in SUM_DIMS if d in order[phase + 1 :]]
            rest = (RING,) * len(open_dims)
            if phase == 2:
                bufs += [(half, cols), (part_rows - half, cols)]
            else:
                bufs += [tuple(2 if d == order[phase + 1] else RING for d in open_dims) + (part_rows, cols)] * 2
            bufs += [rest + (part_rows, cols)] * 2

    def kernel(terms, mid, out, total, other, *rest):
        row_sum_kernel(terms, mid, out, total, other, rest[:36], *rest[36:])

    return pl.pallas_call(
        kernel,
        out_shape=jax.ShapeDtypeStruct((rows, cols), bf16),
        in_specs=[ANY, WHOLE],
        out_specs=ANY,
        scratch_shapes=[
            pltpu.VMEM((RING, RING, RING, rows, cols), bf16),
            pltpu.VMEM((RING, RING, RING, rows, cols), bf16),
        ]
        + [pltpu.VMEM(shape, bf16) for shape in bufs]
        + [
            pltpu.VMEM((rows, cols), bf16),
            pltpu.SemaphoreType.DMA((n,)),
            pltpu.SemaphoreType.DMA((n,)),
            pltpu.SemaphoreType.DMA((13,)),
        ],
        compiler_params=pltpu.CompilerParams(
            collective_id=3, has_side_effects=True, vmem_limit_bytes=48 << 20
        ),
        name="row_sum",
    )(terms, mid)


def attend_kernel(where, pages, queries, first, gathered, out, cache, window, zeros, sems):
    span = window.shape[0]
    block = where[0]
    start = where[1]
    slots = cache.shape[0]
    grab = pltpu.make_async_copy(gathered.at[pl.ds(start, span)], window, sems.at[0])
    grab.start()
    zeros[...] = jnp.zeros_like(zeros)

    def page_copy(slot, page):
        return pltpu.make_async_copy(
            gathered.at[page // 8, pl.ds(pl.multiple_of(lax.rem(page, 8) * PAGE, PAGE), PAGE), :],
            cache.at[slot],
            sems.at[1 + slot],
        )

    def empty_copy(slot):
        return pltpu.make_async_copy(zeros, cache.at[slot], sems.at[1 + slot])

    def send(slot, carry):
        page = pages[slot]

        @pl.when(page >= 0)
        def _():
            page_copy(slot, page).start()

        @pl.when(page < 0)
        def _():
            empty_copy(slot).start()

        return carry

    lax.fori_loop(0, slots, send, 0)
    grab.wait()
    rows = queries.shape[0]
    width = span * rows
    held = window[...][:, :rows, :]
    keys = held[:, :, :HEAD_DIM].reshape(width, HEAD_DIM)
    values = held[:, :, HEAD_DIM:].reshape(width, HEAD_DIM)
    key_at = start * rows + lax.broadcasted_iota(jnp.int32, (rows, width), 1)
    query_at = block * rows + lax.broadcasted_iota(jnp.int32, (rows, width), 0)
    allowed = (key_at <= query_at) & (key_at >= first[...])
    for head in range(queries.shape[1] // HEAD_DIM):
        cols = pl.ds(head * HEAD_DIM, HEAD_DIM)
        scores = lax.dot_general(
            queries[:, cols], keys, (((1,), (1,)), ((), ())), preferred_element_type=f32
        ) * (HEAD_DIM**-0.5)
        scores = jnp.where(allowed, scores, masked_score)
        weights = jnp.where(allowed, jnp.exp(scores - jnp.max(scores, axis=1, keepdims=True)), 0.0)
        totals = jnp.sum(weights, axis=1, keepdims=True)
        mixed = jnp.dot(weights.astype(bf16), values, preferred_element_type=f32)
        out[:, cols] = (mixed / totals).astype(bf16)

    def settle(slot, carry):
        empty_copy(slot).wait()
        return carry

    lax.fori_loop(0, slots, settle, 0)


def attend(block, pages, queries, first, gathered):
    blocks = gathered.shape[0]
    span = min(9, blocks)
    start = jnp.clip(block - 8, 0, blocks - span)
    width = gathered.shape[2]
    return pl.pallas_call(
        attend_kernel,
        grid_spec=pltpu.PrefetchScalarGridSpec(
            num_scalar_prefetch=2,
            grid=(1,),
            in_specs=[
                pl.BlockSpec(queries.shape, lambda i, *_: (0, 0)),
                pl.BlockSpec(first.shape, lambda i, *_: (0, 0)),
                ANY,
            ],
            out_specs=(pl.BlockSpec(queries.shape, lambda i, *_: (0, 0)), ANY),
            scratch_shapes=[
                pltpu.VMEM((span,) + gathered.shape[1:], bf16),
                pltpu.VMEM((PAGE, width), bf16),
                pltpu.SemaphoreType.DMA((1 + pages.shape[0],)),
            ],
        ),
        out_shape=(
            jax.ShapeDtypeStruct(queries.shape, bf16),
            jax.ShapeDtypeStruct((pages.shape[0], PAGE, width), bf16),
        ),
        compiler_params=pltpu.CompilerParams(vmem_limit_bytes=32 << 20),
        name="attend",
    )(jnp.stack([block, start]).astype(jnp.int32), pages, queries, first, gathered)


GROUP = 8
PAIR = 2


def expert_kernel(slot_row, slot_col, gates, rows, w_gate, w_up, w_down, out, packed, made):
    tokens = rows.shape[2]
    pair_cap = PAIR * CAP
    n_exp = w_gate.shape[0]
    quarter = rows.shape[3]
    gate_of = []
    for p in range(GROUP // PAIR):
        picks = []
        for e in range(n_exp):
            lane = slot_row[p, e : e + 1, :]
            row = lax.broadcasted_iota(jnp.int32, (pair_cap, PAIR * tokens), 0)
            picks.append(jnp.broadcast_to(lane, row.shape) == row)
        pick = jnp.concatenate(picks, axis=0)
        weight = jnp.concatenate(
            [jnp.broadcast_to(gates[p, e : e + 1, :], (pair_cap, PAIR * tokens)) for e in range(n_exp)], axis=0
        )
        gate_of.append(jnp.sum(jnp.where(pick, weight, 0.0), axis=1, keepdims=True))
        pick = pick.astype(f32).astype(bf16)
        for q in range(RING):
            block = rows[PAIR * p : PAIR * p + PAIR, q].reshape(PAIR * tokens, quarter)
            got = jnp.dot(pick, block, preferred_element_type=f32).astype(bf16)
            for e in range(n_exp):
                packed[e, p * pair_cap : (p + 1) * pair_cap, q * quarter : (q + 1) * quarter] = got[
                    e * pair_cap : (e + 1) * pair_cap
                ]
    for e in range(n_exp):
        x = packed[e]
        gate_term = jnp.dot(x, w_gate[e], preferred_element_type=f32)
        up_term = jnp.dot(x, w_up[e], preferred_element_type=f32)
        act = (gate_term / (1.0 + jnp.exp(-gate_term)) * up_term).astype(bf16)
        scale = jnp.concatenate(
            [gate_of[p][e * pair_cap : (e + 1) * pair_cap] for p in range(GROUP // PAIR)], axis=0
        )
        for q in range(RING):
            down = jnp.dot(act, w_down[e][:, q * quarter : (q + 1) * quarter], preferred_element_type=f32)
            down = (down * scale).astype(bf16)
            for p in range(GROUP // PAIR):
                made[p, e * pair_cap : (e + 1) * pair_cap, q * quarter : (q + 1) * quarter] = down[
                    p * pair_cap : (p + 1) * pair_cap
                ]
    for p in range(GROUP // PAIR):
        spread = []
        for e in range(n_exp):
            col = slot_col[p, :, e : e + 1]
            lane = lax.broadcasted_iota(jnp.int32, (PAIR * tokens, pair_cap), 1)
            spread.append((jnp.broadcast_to(col, lane.shape) == lane).astype(f32))
        spread = jnp.concatenate(spread, axis=1).astype(bf16)
        for q in range(RING):
            back = jnp.dot(spread, made[p, :, q * quarter : (q + 1) * quarter], preferred_element_type=f32)
            out[PAIR * p : PAIR * p + PAIR, q] = back.astype(bf16).reshape(PAIR, tokens, quarter)


def experts(slot_row, slot_col, gates, rows, w_gate, w_up, w_down):
    blocks, _, tokens, quarter = rows.shape
    n_exp, width, ff = w_gate.shape
    pairs = GROUP // PAIR
    pair_cap = PAIR * CAP

    def fixed(shape):
        return pl.BlockSpec(shape, lambda i: (0,) * len(shape), pipeline_mode=pl.Buffered(1))

    return pl.pallas_call(
        expert_kernel,
        grid=(blocks // GROUP,),
        in_specs=[
            pl.BlockSpec((pairs, n_exp, PAIR * tokens), lambda i: (i, 0, 0)),
            pl.BlockSpec((pairs, PAIR * tokens, n_exp), lambda i: (i, 0, 0)),
            pl.BlockSpec((pairs, n_exp, PAIR * tokens), lambda i: (i, 0, 0)),
            pl.BlockSpec((GROUP, RING, tokens, quarter), lambda i: (i, 0, 0, 0)),
            fixed(w_gate.shape),
            fixed(w_up.shape),
            fixed(w_down.shape),
        ],
        out_specs=pl.BlockSpec((GROUP, RING, tokens, quarter), lambda i: (i, 0, 0, 0)),
        out_shape=jax.ShapeDtypeStruct(rows.shape, bf16),
        scratch_shapes=[
            pltpu.VMEM((n_exp, GROUP * CAP, width), bf16),
            pltpu.VMEM((pairs, n_exp * pair_cap, width), bf16),
        ],
        compiler_params=pltpu.CompilerParams(vmem_limit_bytes=56 << 20),
        name="experts",
    )(slot_row, slot_col, gates, rows, w_gate, w_up, w_down)


def rms_norm(values, gain_vec):
    widened = values.astype(f32)
    factor = lax.rsqrt(jnp.mean(widened * widened, axis=-1, keepdims=True) + epsilon)
    return (widened * factor * gain_vec).astype(bf16)


def rotate(values, position):
    half_dim = HEAD_DIM // 2
    inverse = rope_base ** (-2.0 * jnp.arange(half_dim, dtype=f32) / HEAD_DIM)
    angles = position.astype(f32)[:, None] * inverse[None, :]
    cosine, sine = jnp.cos(angles), jnp.sin(angles)
    heads = []
    for head in range(values.shape[1] // HEAD_DIM):
        one = values[:, head * HEAD_DIM : (head + 1) * HEAD_DIM]
        first, second = one[:, :half_dim], one[:, half_dim:]
        heads += [first * cosine - second * sine, second * cosine + first * sine]
    return jnp.concatenate(heads, axis=1).astype(bf16)


def segment_start(seg_lengths, positions):
    count = seg_lengths.shape[0]
    earlier = jnp.arange(count)[None, :] < jnp.arange(count)[:, None]
    starts = jnp.sum(jnp.where(earlier, seg_lengths[None, :], 0), axis=1)
    return jnp.max(jnp.where(starts[None, :] <= positions[:, None], starts[None, :], 0), axis=1)


def local(
    hidden, gain_attn, w_query, w_key, w_value, w_out, gain_moe, expert_ids, expert_gates,
    w_gate, w_up, w_down, seg_lengths, slot_page,
):
    tok_rows, model_width = hidden.shape
    shard_count = lax.axis_size("seq")
    shard_index = lax.axis_index("seq")
    tensor_index = lax.axis_index("tp")
    quarter = model_width // RING
    positions = shard_index * tok_rows + jnp.arange(tok_rows, dtype=jnp.int32)
    seg_first = segment_start(seg_lengths, positions)
    offsets = positions - seg_first
    normed = rms_norm(hidden, gain_attn)
    queries = rotate(jnp.dot(normed, w_query, preferred_element_type=f32), offsets)
    keys_rot = rotate(jnp.dot(normed, w_key, preferred_element_type=f32), offsets)
    values = jnp.dot(normed, w_value, preferred_element_type=f32).astype(bf16)
    gate_high = expert_gates.astype(bf16)
    gate_low = (expert_gates - gate_high.astype(f32)).astype(bf16)
    routing = jnp.concatenate([expert_ids.astype(bf16), gate_high, gate_low], axis=1).T
    routing = jnp.pad(routing.reshape(3 * TOP * tok_rows // 256, 256), ((0, 7), (0, 0)))
    sent = jnp.concatenate([jnp.concatenate([keys_rot, values], axis=1), routing], axis=0)
    gathered = kv_gather(sent).reshape(shard_count, tok_rows + 16, 256)
    slot_count = slot_page.shape[0] // shard_count
    own_slots = lax.dynamic_slice_in_dim(slot_page, shard_index * slot_count, slot_count)
    attended, kv_cache = attend(shard_index, own_slots, queries, seg_first[:, None], gathered)
    table = gathered[:, tok_rows : tok_rows + 9, :].reshape(shard_count, 3 * TOP, tok_rows).astype(f32)
    n_exp = w_gate.shape[0]
    mine = shard_index * n_exp + jnp.arange(n_exp)
    hits = table[:, None, :TOP, :] == mine[None, :, None, None].astype(f32)
    gates = jnp.sum(
        jnp.where(hits, table[:, None, TOP : 2 * TOP, :] + table[:, None, 2 * TOP :, :], 0.0), axis=2
    )
    named = jnp.any(hits, axis=2)
    before = (jnp.arange(tok_rows)[:, None] < jnp.arange(tok_rows)[None, :]).astype(bf16)
    rank = jnp.einsum("set,tu->seu", named.astype(bf16), before, preferred_element_type=f32)
    pair_at = (jnp.arange(shard_count) % PAIR * CAP)[:, None, None]
    slot = jnp.where(named, rank.astype(jnp.int32) + pair_at, -1)

    def paired(values):
        return values.reshape(shard_count // PAIR, PAIR, n_exp, tok_rows).swapaxes(1, 2).reshape(
            shard_count // PAIR, n_exp, PAIR * tok_rows
        )

    slot_row, gates = paired(slot), paired(gates)
    slot_col = slot_row.swapaxes(1, 2)
    terms = jnp.stack(
        [
            jnp.dot(attended, w_out[:, q * quarter : (q + 1) * quarter], preferred_element_type=f32)
            for q in range(RING)
        ]
    ).astype(bf16)
    own_hidden = lax.dynamic_slice_in_dim(hidden, tensor_index * quarter, quarter, 1)
    own_gain = lax.dynamic_slice_in_dim(gain_moe, tensor_index * quarter, quarter)[None, :]
    rows, mid = row_gather(terms, own_hidden, own_gain)
    made = experts(
        slot_row, slot_col, gates, rows.reshape(shard_count, RING, tok_rows, quarter), w_gate, w_up, w_down
    )
    return (row_sum(made.reshape(rows.shape), mid), kv_cache)


def solution(mesh):
    placed = (
        P("seq", None),
        P(),
        P(None, "tp"),
        P(None, "tp"),
        P(None, "tp"),
        P("tp", None),
        P(),
        P("seq", None),
        P("seq", None),
        P("seq", None, "tp"),
        P("seq", None, "tp"),
        P("seq", "tp", None),
        P(),
        P(),
    )
    return jax.shard_map(
        local,
        mesh=mesh,
        in_specs=placed,
        out_specs=(P("seq", "tp"), P("seq", None, "tp")),
        check_vma=False,
    )
```

```python
import functools

import jax
import jax.numpy as jnp
from jax import lax
from jax.experimental import pallas as pl
from jax.experimental.pallas import tpu as pltpu
from jax.sharding import PartitionSpec as P

HEAD_DIM = 128
TOP = 6
PAGE = 16
CAP = 24
RING = 4
MESH = pl.DeviceIdType.MESH
ANY = pl.BlockSpec(memory_space=pl.ANY)
WHOLE = pl.BlockSpec(memory_space=pltpu.VMEM)
epsilon = 1e-05
rope_base = 500000.0
masked_score = -1e30
bf16 = jnp.bfloat16
f32 = jnp.float32


def my_place():
    index = lax.axis_index("seq")
    return {
        "x": index // 8,
        "z": lax.rem(index // 2, RING),
        "c": lax.rem(index, 2),
        "y": lax.axis_index("tp"),
    }


def device_at(place):
    return ((place["x"] * RING + place["z"]) * 2 + place["c"], place["y"])


def moved(place, axis, step):
    size = 2 if axis == "c" else RING
    other = dict(place)
    other[axis] = lax.rem(place[axis] + step + size, size)
    return other


def enter(places):
    barrier = pltpu.get_barrier_semaphore()
    for place in places:
        pl.semaphore_signal(barrier, inc=1, device_id=device_at(place), device_id_type=MESH)
    pl.semaphore_wait(barrier, len(places))


class Links:
    def __init__(self, send_sem, recv_sem):
        self.send_sem, self.recv_sem, self.count = send_sem, recv_sem, 0
        self.started = []

    def push(self, src, dst, place):
        copy = pltpu.make_async_remote_copy(
            src_ref=src,
            dst_ref=dst,
            send_sem=self.send_sem.at[self.count],
            recv_sem=self.recv_sem.at[self.count],
            device_id=device_at(place),
            device_id_type=MESH,
        )
        self.count += 1
        copy.start()
        self.started.append(copy)
        return copy

    def finish(self):
        for copy in self.started:
            copy.wait_send()


def torus_gather(me, dims, parts, src, out, links, local_sem, beside=None):
    sibling = moved(me, "c", 1)

    def at(where, row0, rows):
        return out.at[tuple(where[d] for d in dims) + (pl.ds(row0, rows), slice(None))]

    own = {d: me[d] for d in dims}
    local = pltpu.make_async_copy(src, at(own, 0, src.shape[0]), local_sem)
    local.start()
    to_sibling = [links.push(src, at(own, 0, src.shape[0]), sibling)]
    for phase in range(len(parts[0][3])):
        if phase == 1:
            local.wait()
        live = []
        for row0, rows, half, order in parts:
            axis = order[phase]
            base = dict(own)
            for done in order[:phase]:
                base[done] = slice(None)
            whole = at(base, row0, rows)
            source = src.at[pl.ds(row0, rows), :] if phase == 0 else whole
            up = links.push(source, whole, moved(me, axis, 1))
            down = links.push(source, whole, moved(me, axis, -1))
            live.append((row0, rows, half, order, axis, base, up, down))
        if phase == 0 and beside is not None:
            beside()
        forwarded = []
        for row0, rows, half, order, axis, base, up, down in live:
            for copy, step in ((up, 1), (down, -1)):
                copy.wait_recv()
                got = dict(base)
                got[axis] = moved(me, axis, -step)[axis]
                if phase == 0:
                    r0, rn = (row0, half) if step == 1 else (row0 + half, rows - half)
                    piece = at(got, r0, rn)
                else:
                    cut = dict(got)
                    cut[order[0]] = pl.ds(0, 2) if step == 1 else pl.ds(2, 2)
                    piece = at(cut, row0, rows)
                forwarded.append(links.push(piece, piece, moved(me, axis, step)))
                there = at(got, row0, rows)
                to_sibling.append(links.push(there, there, sibling))
        for n, (row0, rows, half, order, axis, base, up, down) in enumerate(live):
            forwarded[2 * n].wait_recv()
            forwarded[2 * n + 1].wait_recv()
            got = dict(base)
            got[axis] = moved(me, axis, 2)[axis]
            there = at(got, row0, rows)
            to_sibling.append(links.push(there, there, sibling))
    for copy in to_sibling:
        copy.wait_recv()


def copies_of_gather(parts):
    phases = len(parts[0][3])
    return 1 + phases * len(parts) * 7


KV_PARTS = ((0, 80, 48, ("x", "z")), (80, 64, 32, ("z", "x")))
UNIT = (16, 128)
ROW_PARTS = (
    (0, 14, ("z", "y", "x")),
    (14, 13, ("y", "x", "z")),
    (27, 13, ("x", "z", "y")),
)
STREAMS = ((0, 1), (1, -1), (-1, 1), (2, -1))


def wave(stages):
    for stage in range(stages):
        for n in range(len(STREAMS)):
            yield stage, n


def to_units(values):
    rows, cols = values.shape
    return [
        values[:, j * 128 : (j + 1) * 128].reshape(rows // 16, 16, 128) for j in range(cols // 128)
    ]


def from_units(units, rows):
    group = rows // 16
    tiles = [units[j * group : (j + 1) * group].reshape(rows, 128) for j in range(units.shape[0] // group)]
    return jnp.concatenate(tiles, axis=1)


def stream_gather(me, src, out, links, local_sem):
    sibling = moved(me, "c", 1)

    def at(where, first, count):
        return out.at[where["x"], where["z"], where["c"], where["y"], pl.ds(first, count)]

    local = pltpu.make_async_copy(src, at(me, 0, src.shape[0]), local_sem)
    local.start()
    echo = []
    landed = {}
    for p, (u0, n, order) in enumerate(ROW_PARTS):
        piece = src.at[pl.ds(u0, n)]
        for step in (1, -1, 2):
            landed[p, step] = links.push(piece, at(me, u0, n), moved(me, order[0], step))
    state = {}

    def region(p, stream, ring, step):
        u0, n, order = ROW_PARTS[p]
        where = dict(me)
        where[order[0]] = moved(me, order[0], STREAMS[stream][0])[order[0]]
        if ring == 2:
            where[order[1]] = slice(None)
        where[order[ring]] = moved(me, order[ring], step)[order[ring]]
        return at(where, u0, n)

    def relay(ref):
        echo.append(links.push(ref, ref, sibling))

    for stage, stream in wave(6):
        step, way = STREAMS[stream]
        for p, (u0, n, order) in enumerate(ROW_PARTS):
            ring = 1 + stage // 3
            axis = order[ring]
            if stage % 3 == 0:
                if stage == 0:
                    if step == 0:
                        if p == 0:
                            local.wait()
                    else:
                        landed[p, -step if step != 2 else 2].wait_recv()
                else:
                    state[p, stream, 1, "far"].wait_recv()
                    whole = dict(me)
                    whole[order[0]] = moved(me, order[0], step)[order[0]]
                    whole[order[1]] = slice(None)
                    relay(at(whole, u0, n))
                own = region(p, stream, ring, 0)
                for w in (1, -1):
                    state[p, stream, ring, w] = links.push(own, own, moved(me, axis, w))
            elif stage % 3 == 1:
                state[p, stream, ring, way].wait_recv()
                near = region(p, stream, ring, -way)
                state[p, stream, ring, "far"] = links.push(near, near, moved(me, axis, way))
                state[p, stream, ring, -way].wait_recv()
                if ring == 2:
                    relay(near)
                    relay(region(p, stream, ring, way))
            elif ring == 2:
                state[p, stream, ring, "far"].wait_recv()
                relay(region(p, stream, ring, 2))
    for copy in echo:
        copy.wait_recv()


STREAM_COPIES = len(ROW_PARTS) * (3 + 4 * (3 + 4 + 3))


def turn(one, cosine, sine):
    return one * cosine + pltpu.roll(one, HEAD_DIM // 2, 1) * sine


def front_kernel(
    lengths, hidden, gain, inverse, routing, w_query, w_key, w_value,
    gathered, queries, first, sent, wq, wk, wv, normed, send_sem, recv_sem, local_sem,
):
    me = my_place()
    loads = [
        pltpu.make_async_copy(src, dst, local_sem.at[1 + n])
        for n, (src, dst) in enumerate(((w_key, wk), (w_value, wv), (w_query, wq)))
    ]
    for load in loads:
        load.start()
    rows = hidden.shape[0]
    block = (me["x"] * RING + me["z"]) * 2 + me["c"]
    at = block * rows + lax.broadcasted_iota(jnp.int32, (rows, 1), 0)
    begin = jnp.zeros((rows, 1), jnp.int32)
    running = lengths[0]
    for n in range(1, lengths.shape[0]):
        begin = jnp.where(at >= running, running, begin)
        running = running + lengths[n]
    first[...] = begin
    angles = (at - begin).astype(f32) * inverse[...]
    cosine = jnp.cos(angles)
    lane = lax.broadcasted_iota(jnp.int32, angles.shape, 1)
    sine = jnp.where(lane < HEAD_DIM // 2, -jnp.sin(angles), jnp.sin(angles))
    wide = hidden[...].astype(f32)
    factor = lax.rsqrt(jnp.mean(wide * wide, axis=1, keepdims=True) + epsilon)
    normed[...] = (wide * factor * gain[...]).astype(bf16)
    turned = routing[...].T
    sent[rows : rows + 16, :HEAD_DIM] = turned[:16].astype(bf16)
    sent[rows : rows + 16, HEAD_DIM:] = turned[16:32].astype(bf16)
    loads[0].wait()
    key = jnp.dot(normed[...], wk[...], preferred_element_type=f32)
    sent[:rows, :HEAD_DIM] = turn(key, cosine, sine).astype(bf16)
    loads[1].wait()
    sent[:rows, HEAD_DIM:] = jnp.dot(normed[...], wv[...], preferred_element_type=f32).astype(bf16)
    enter([moved(me, a, s) for a in ("x", "z") for s in (1, -1)] + [moved(me, "c", 1)])
    links = Links(send_sem, recv_sem)

    def beside():
        loads[2].wait()
        raw = jnp.dot(normed[...], wq[...], preferred_element_type=f32)
        for head in range(raw.shape[1] // HEAD_DIM):
            cols = slice(head * HEAD_DIM, (head + 1) * HEAD_DIM)
            queries[:, cols] = turn(raw[:, cols], cosine, sine).astype(bf16)

    torus_gather(me, ("x", "z", "c"), KV_PARTS, sent, gathered, links, local_sem.at[0], beside)
    links.finish()


def front(lengths, hidden, gain, inverse, routing, w_query, w_key, w_value):
    n = copies_of_gather(KV_PARTS)
    rows = hidden.shape[0]
    width = w_key.shape[1] + w_value.shape[1]
    return pl.pallas_call(
        front_kernel,
        out_shape=(
            jax.ShapeDtypeStruct((RING, RING, 2, rows + 16, width), bf16),
            jax.ShapeDtypeStruct((rows, w_query.shape[1]), bf16),
            jax.ShapeDtypeStruct((rows, 1), jnp.int32),
        ),
        in_specs=[pl.BlockSpec(memory_space=pltpu.SMEM)] + [WHOLE] * 4 + [ANY] * 3,
        out_specs=(ANY, WHOLE, WHOLE),
        scratch_shapes=[
            pltpu.VMEM((rows + 16, width), bf16),
            pltpu.VMEM(w_query.shape, bf16),
            pltpu.VMEM(w_key.shape, bf16),
            pltpu.VMEM(w_value.shape, bf16),
            pltpu.VMEM(hidden.shape, bf16),
            pltpu.SemaphoreType.DMA((n,)),
            pltpu.SemaphoreType.DMA((n,)),
            pltpu.SemaphoreType.DMA((4,)),
        ],
        compiler_params=pltpu.CompilerParams(
            collective_id=1, has_side_effects=True, vmem_limit_bytes=48 << 20
        ),
        name="front",
    )(lengths, hidden, gain, inverse, routing, w_query, w_key, w_value)


def row_gather_kernel(
    terms, hidden, gain, out, mid, heard, squares, mid_v, row_v, send_sem, recv_sem, local_sem
):
    me = my_place()
    width = mid.shape[1]
    mine = pl.ds(pl.multiple_of(me["y"] * width, 128), width)
    peers = [moved(me, "y", s) for s in (1, 2, 3)]
    enter([moved(me, a, s) for a in ("x", "z") for s in (1, -1, 2)] + [moved(me, "c", 1)] + peers)
    links = Links(send_sem, recv_sem)
    sent = [
        links.push(terms.at[peer["y"]], heard.at[n], peer) for n, peer in enumerate(peers)
    ]
    total = terms[me["y"]].astype(f32)
    for n in range(3):
        sent[n].wait_recv()
        total = total + heard[n].astype(f32)
    mid_now = (hidden[:, mine].astype(f32) + total).astype(bf16)
    mid_v[...] = mid_now
    wide = mid_now.astype(f32)
    ours = jnp.sum(wide * wide, axis=1, keepdims=True)
    squares[3] = jnp.broadcast_to(ours, (ours.shape[0], 128)).T[:8]
    told = [links.push(squares.at[3], squares.at[n], peer) for n, peer in enumerate(peers)]
    whole = squares[3]
    for n in range(3):
        told[n].wait_recv()
        whole = whole + squares[n]
    whole = jnp.broadcast_to(whole[:1], (128, 128)).T[:, :1]
    factor = lax.rsqrt(whole * (1.0 / (RING * wide.shape[1])) + epsilon)
    ready = (wide * factor * gain[:, mine]).astype(bf16)
    for j, tile in enumerate(to_units(ready)):
        row_v[j * tile.shape[0] : (j + 1) * tile.shape[0]] = tile
    keep = pltpu.make_async_copy(mid_v, mid, local_sem.at[1])
    keep.start()
    stream_gather(me, row_v, out, links, local_sem.at[0])
    keep.wait()
    links.finish()


def row_gather(terms, hidden, gain):
    n = 6 + STREAM_COPIES
    rows, cols = terms.shape[1:]
    units = rows * cols // (UNIT[0] * UNIT[1])
    return pl.pallas_call(
        row_gather_kernel,
        out_shape=(
            jax.ShapeDtypeStruct((RING, RING, 2, RING, units) + UNIT, bf16),
            jax.ShapeDtypeStruct((rows, cols), bf16),
        ),
        in_specs=[WHOLE, WHOLE, WHOLE],
        out_specs=(ANY, ANY),
        scratch_shapes=[
            pltpu.VMEM((3, rows, cols), bf16),
            pltpu.VMEM((4, 8, rows), f32),
            pltpu.VMEM((rows, cols), bf16),
            pltpu.VMEM((units,) + UNIT, bf16),
            pltpu.SemaphoreType.DMA((n,)),
            pltpu.SemaphoreType.DMA((n,)),
            pltpu.SemaphoreType.DMA((2,)),
        ],
        compiler_params=pltpu.CompilerParams(
            collective_id=2, has_side_effects=True, vmem_limit_bytes=48 << 20
        ),
        name="row_gather",
    )(terms, hidden, gain)


SUM_DIMS = ("x", "z", "y")
SUM_STREAMS = ((2, 1), (1, -1), (-1, 1), (0, -1))


def row_sum_kernel(terms, mid, out, total, other, bufs, out_v, send_sem, recv_sem, local_sem):
    me = my_place()
    sibling = moved(me, "c", 1)
    enter([moved(me, a, s) for a in ("x", "z", "y") for s in (1, -1, 2)] + [sibling])
    links = Links(send_sem, recv_sem)

    def held(ref, where, u0, n):
        return ref.at[tuple(where[d] for d in SUM_DIMS) + (pl.ds(u0, n),)]

    def place(p, stream, **free):
        order = ROW_PARTS[p][2]
        where = dict(me)
        where[order[0]] = moved(me, order[0], SUM_STREAMS[stream][0])[order[0]]
        where.update(free)
        return where

    first = {}
    for stream in range(4):
        for p, (u0, n, order) in enumerate(ROW_PARTS):
            where = place(p, stream, **{order[1]: slice(None), order[2]: slice(None)})
            slot = stream * 3 + p
            keep = pltpu.make_async_copy(
                terms.at[where["x"], where["z"], me["c"], where["y"], pl.ds(u0, n)],
                held(total, where, u0, n),
                local_sem.at[slot],
            )
            keep.start()
            push = links.push(
                terms.at[where["x"], where["z"], sibling["c"], where["y"], pl.ds(u0, n)],
                held(other, where, u0, n),
                sibling,
            )
            first[p, stream] = (keep, push)

    def add(where, u0, n, buf, lead):
        span = pl.ds(u0, n)
        if lead is None:
            index = tuple(where[d] for d in SUM_DIMS) + (span,)
            total[index] = total[index] + buf[...]
            return

        def one(k, carry):
            index = tuple(k if d == lead else where[d] for d in SUM_DIMS) + (span,)
            total[index] = total[index] + buf[k]
            return carry

        lax.fori_loop(0, RING, one, 0)

    state = {}
    for stage, stream in wave(6):
        step, way = SUM_STREAMS[stream]
        for p, (u0, n, order) in enumerate(ROW_PARTS):
            if stage == 0:
                keep, push = first[p, stream]
                keep.wait()
                push.wait_recv()
                where = place(p, stream)
                span = pl.ds(u0, n)

                def one(k, carry, where=where, span=span, order=order):
                    spot = {order[1]: k // RING, order[2]: lax.rem(k, RING)}
                    index = tuple(spot.get(d, where[d]) for d in SUM_DIMS) + (span,)
                    total[index] = total[index] + other[index]
                    return carry

                lax.fori_loop(0, RING * RING, one, 0)
            ring = 2 - stage // 3
            axis = order[ring]
            lead = order[1] if ring == 2 else None
            free = {order[1]: slice(None)} if ring == 2 else {}
            far, near, back = bufs[((2 - ring) * 4 + stream) * 3 + p]
            at = lambda s: place(p, stream, **free, **{axis: moved(me, axis, s)[axis]})
            if stage % 3 == 0:
                state[p, stream, ring, "far"] = links.push(held(total, at(2), u0, n), far, moved(me, axis, way))
                state[p, stream, ring, "back"] = links.push(held(total, at(-way), u0, n), back, moved(me, axis, -way))
            elif stage % 3 == 1:
                state[p, stream, ring, "far"].wait_recv()
                add(at(way), u0, n, far, lead)
                state[p, stream, ring, "near"] = links.push(held(total, at(way), u0, n), near, moved(me, axis, way))
            else:
                state[p, stream, ring, "back"].wait_recv()
                add(at(0), u0, n, back, lead)
                state[p, stream, ring, "near"].wait_recv()
                add(at(0), u0, n, near, lead)
                if ring == 1 and step != 0:
                    state[p, stream, "last"] = links.push(
                        held(total, place(p, stream), u0, n), bufs[24 + stream * 3 + p][0], moved(me, order[0], step)
                    )
    for stream in range(3):
        for p, (u0, n, order) in enumerate(ROW_PARTS):
            state[p, stream, "last"].wait_recv()
            add(me, u0, n, bufs[24 + stream * 3 + p][0], None)
    done = from_units(total[me["x"], me["z"], me["y"]], out.shape[0])
    out_v[...] = (mid[...].astype(f32) + done.astype(f32)).astype(bf16)
    write = pltpu.make_async_copy(out_v, out, local_sem.at[12])
    write.start()
    write.wait()
    links.finish()


def row_sum(terms, mid):
    rows, cols = mid.shape
    units = terms.shape[4]
    n = 12 + 3 * (4 * 6 + 3)
    bufs = []
    for ring in (2, 1):
        for stream in range(4):
            for _, count, _ in ROW_PARTS:
                bufs += [((RING,) if ring == 2 else ()) + (count,) + UNIT] * 3
    for stream in range(3):
        for _, count, _ in ROW_PARTS:
            bufs += [(count,) + UNIT]

    def kernel(terms, mid, out, total, other, *rest):
        flat, rest = rest[: len(bufs)], rest[len(bufs) :]
        sets = [flat[3 * k : 3 * k + 3] for k in range(24)] + [flat[72 + k : 73 + k] for k in range(9)]
        row_sum_kernel(terms, mid, out, total, other, sets, *rest)

    return pl.pallas_call(
        kernel,
        out_shape=jax.ShapeDtypeStruct((rows, cols), bf16),
        in_specs=[ANY, WHOLE],
        out_specs=ANY,
        scratch_shapes=[
            pltpu.VMEM((RING, RING, RING, units) + UNIT, bf16),
            pltpu.VMEM((RING, RING, RING, units) + UNIT, bf16),
        ]
        + [pltpu.VMEM(shape, bf16) for shape in bufs]
        + [
            pltpu.VMEM((rows, cols), bf16),
            pltpu.SemaphoreType.DMA((n,)),
            pltpu.SemaphoreType.DMA((n,)),
            pltpu.SemaphoreType.DMA((13,)),
        ],
        compiler_params=pltpu.CompilerParams(
            collective_id=3, has_side_effects=True, vmem_limit_bytes=48 << 20
        ),
        name="row_sum",
    )(terms, mid)


def attend_kernel(
    where, pages, queries, first, gathered, w_out, terms, cache, slot, gates,
    window, meta, wo, zeros, attended, sems, page_sems,
):
    span = window.shape[0]
    block, start = where[0], where[1]
    slots = cache.shape[0]
    rows = queries.shape[0]
    grab = pltpu.make_async_copy(gathered.at[pl.ds(start, span)], window, sems.at[0])
    grab.start()
    note = pltpu.make_async_copy(gathered.at[:, pl.ds(rows, 16), :], meta, sems.at[1])
    note.start()
    load = pltpu.make_async_copy(w_out, wo, sems.at[2])
    load.start()
    zeros[...] = jnp.zeros_like(zeros)

    def page_copy(n, page):
        return pltpu.make_async_copy(
            gathered.at[page // 8, pl.ds(pl.multiple_of(lax.rem(page, 8) * PAGE, PAGE), PAGE), :],
            cache.at[n],
            page_sems.at[n],
        )

    def empty_copy(n):
        return pltpu.make_async_copy(zeros, cache.at[n], page_sems.at[n])

    def send(n, carry):
        page = pages[n]

        @pl.when(page >= 0)
        def _():
            page_copy(n, page).start()

        @pl.when(page < 0)
        def _():
            empty_copy(n).start()

        return carry

    lax.fori_loop(0, slots, send, 0)
    grab.wait()
    width = span * rows
    held = window[...][:, :rows, :]
    keys = held[:, :, :HEAD_DIM].reshape(width, HEAD_DIM)
    values = held[:, :, HEAD_DIM:].reshape(width, HEAD_DIM)
    key_at = start * rows + lax.broadcasted_iota(jnp.int32, (rows, width), 1)
    query_at = block * rows + lax.broadcasted_iota(jnp.int32, (rows, width), 0)
    allowed = (key_at <= query_at) & (key_at >= first[...])
    for head in range(queries.shape[1] // HEAD_DIM):
        cols = pl.ds(head * HEAD_DIM, HEAD_DIM)
        scores = lax.dot_general(
            queries[:, cols], keys, (((1,), (1,)), ((), ())), preferred_element_type=f32
        ) * (HEAD_DIM**-0.5)
        scores = jnp.where(allowed, scores, masked_score)
        weights = jnp.where(allowed, jnp.exp(scores - jnp.max(scores, axis=1, keepdims=True)), 0.0)
        totals = jnp.sum(weights, axis=1, keepdims=True)
        mixed = jnp.dot(weights.astype(bf16), values, preferred_element_type=f32)
        attended[:, cols] = (mixed / totals).astype(bf16)
    load.wait()
    out_width = terms.shape[2]
    for half in range(2):
        cols = slice(2 * half * out_width, 2 * (half + 1) * out_width)
        part = jnp.dot(attended[...], wo[:, cols], preferred_element_type=f32).astype(bf16)
        terms[2 * half] = part[:, :out_width]
        terms[2 * half + 1] = part[:, out_width:]
    note.wait()
    ids = meta[:, :TOP, :HEAD_DIM].astype(f32)
    weight = meta[:, TOP : 2 * TOP, :HEAD_DIM].astype(f32) + meta[:, TOP : 2 * TOP, HEAD_DIM:].astype(f32)
    blocks = meta.shape[0]
    earlier = lax.broadcasted_iota(jnp.int32, (rows, rows), 0) < lax.broadcasted_iota(jnp.int32, (rows, rows), 1)
    earlier = earlier.astype(f32).astype(bf16)
    odd = lax.rem(lax.broadcasted_iota(jnp.int32, (blocks, rows), 0), PAIR).astype(f32) * CAP
    n_exp = slot.shape[0]
    for e in range(n_exp):
        hits = ids == (block * n_exp + e).astype(f32)
        named = jnp.max(hits.astype(f32), axis=1)
        rank = jnp.dot(named.astype(bf16), earlier, preferred_element_type=f32)
        place = jnp.where(named > 0.0, rank + odd, -1.0)
        slot[e] = jnp.concatenate([place.reshape(blocks // PAIR, PAIR, rows)[:, b] for b in range(PAIR)], axis=1)
        share = jnp.sum(jnp.where(hits, weight, 0.0), axis=1)
        gates[e] = jnp.concatenate([share.reshape(blocks // PAIR, PAIR, rows)[:, b] for b in range(PAIR)], axis=1)

    def settle(n, carry):
        empty_copy(n).wait()
        return carry

    lax.fori_loop(0, slots, settle, 0)


def attend(block, pages, queries, first, gathered, w_out, n_exp):
    blocks = gathered.shape[0]
    span = min(9, blocks)
    start = jnp.clip(block - 8, 0, blocks - span)
    width = gathered.shape[2]
    rows = queries.shape[0]
    terms = (RING, rows, w_out.shape[1] // RING)
    slot = (n_exp, blocks // PAIR, PAIR * rows)

    def whole(shape):
        return pl.BlockSpec(shape, lambda i, *_: (0,) * len(shape))

    return pl.pallas_call(
        attend_kernel,
        grid_spec=pltpu.PrefetchScalarGridSpec(
            num_scalar_prefetch=2,
            grid=(1,),
            in_specs=[whole(queries.shape), whole(first.shape), ANY, ANY],
            out_specs=(whole(terms), ANY, whole(slot), whole(slot)),
            scratch_shapes=[
                pltpu.VMEM((span,) + gathered.shape[1:], bf16),
                pltpu.VMEM((blocks, 16, width), bf16),
                pltpu.VMEM(w_out.shape, bf16),
                pltpu.VMEM((PAGE, width), bf16),
                pltpu.VMEM(queries.shape, bf16),
                pltpu.SemaphoreType.DMA((3,)),
                pltpu.SemaphoreType.DMA((pages.shape[0],)),
            ],
        ),
        out_shape=(
            jax.ShapeDtypeStruct(terms, bf16),
            jax.ShapeDtypeStruct((pages.shape[0], PAGE, width), bf16),
            jax.ShapeDtypeStruct(slot, f32),
            jax.ShapeDtypeStruct(slot, f32),
        ),
        compiler_params=pltpu.CompilerParams(vmem_limit_bytes=48 << 20),
        name="attend",
    )(jnp.stack([block, start]).astype(jnp.int32), pages, queries, first, gathered, w_out)


PAIR = 2


def expert_kernel(slot, gates, rows, w_gate, w_up, w_down, out, packed, scale, wgu, wd, sems):
    step = pl.program_id(0)
    groups = 8
    tokens = groups * UNIT[0]
    tiles = rows.shape[4] // groups
    quarter = tiles * UNIT[1]
    pair_cap = PAIR * CAP
    n_exp, _, ff = w_gate.shape
    loads = [
        pltpu.make_async_copy(src, dst, sems.at[n])
        for n, (src, dst) in enumerate(
            ((w_gate, wgu.at[:, :, pl.ds(0, ff)]), (w_up, wgu.at[:, :, pl.ds(ff, ff)]), (w_down, wd))
        )
    ]

    @pl.when(step == 0)
    def _():
        for load in loads:
            load.start()

    row = lax.broadcasted_iota(jnp.int32, (pair_cap, PAIR * tokens), 0).astype(f32)
    picks = []
    for z in range(RING):
        span = slice(z * pair_cap, (z + 1) * pair_cap)
        same = [
            jnp.broadcast_to(slot[e, pl.ds(step * RING + z, 1), :], row.shape) == row for e in range(n_exp)
        ]
        for e in range(n_exp):
            scale[e, span, :] = jnp.sum(
                jnp.where(same[e], gates[e, pl.ds(step * RING + z, 1), :], 0.0), axis=1, keepdims=True
            )
        picks.append(jnp.concatenate([m.astype(f32) for m in same], axis=0).astype(bf16))
        for h in range(2):
            parts = []
            for k in range(2):
                for j in range(tiles):
                    units = slice(j * groups, (j + 1) * groups)
                    parts.append(rows[0, z, :, 2 * h + k, units].reshape(PAIR * tokens, 128))
            got = jnp.dot(picks[z], jnp.concatenate(parts, axis=1), preferred_element_type=f32).astype(bf16)
            for e in range(n_exp):
                packed[e, span, 2 * h * quarter : 2 * (h + 1) * quarter] = got[e * pair_cap : (e + 1) * pair_cap]

    @pl.when(step == 0)
    def _():
        for load in loads:
            load.wait()

    for e in range(n_exp):
        both = jnp.dot(packed[e], wgu[e], preferred_element_type=f32)
        gate_term, up_term = both[:, :ff], both[:, ff:]
        act = (gate_term / (1.0 + jnp.exp(-gate_term)) * up_term).astype(bf16)
        for h in range(2):
            cols = slice(2 * h * quarter, 2 * (h + 1) * quarter)
            down = jnp.dot(act, wd[e, :, cols], preferred_element_type=f32)
            packed[e, :, cols] = (down * scale[e]).astype(bf16)
    for z in range(RING):
        span = slice(z * pair_cap, (z + 1) * pair_cap)
        for h in range(2):
            cols = slice(2 * h * quarter, 2 * (h + 1) * quarter)
            made = jnp.concatenate([packed[e, span, cols] for e in range(n_exp)], axis=0)
            back = lax.dot_general(picks[z], made, (((0,), (0,)), ((), ())), preferred_element_type=f32).astype(bf16)
            for k in range(2):
                for j in range(tiles):
                    n = k * tiles + j
                    out[0, z, :, 2 * h + k, j * groups : (j + 1) * groups] = back[:, n * 128 : (n + 1) * 128].reshape(
                        PAIR, groups, *UNIT
                    )


def experts(slot, gates, rows, w_gate, w_up, w_down):
    n_exp, width, ff = w_gate.shape
    taken = (n_exp, RING * PAIR * CAP)
    whole = pl.BlockSpec(slot.shape, lambda i: (0, 0, 0))
    some = pl.BlockSpec((1,) + rows.shape[1:], lambda i: (i,) + (0,) * (len(rows.shape) - 1))
    return pl.pallas_call(
        expert_kernel,
        grid=(RING,),
        in_specs=[whole, whole, some, ANY, ANY, ANY],
        out_specs=some,
        out_shape=jax.ShapeDtypeStruct(rows.shape, bf16),
        scratch_shapes=[
            pltpu.VMEM(taken + (width,), bf16),
            pltpu.VMEM(taken + (1,), f32),
            pltpu.VMEM((n_exp, width, 2 * ff), bf16),
            pltpu.VMEM(w_down.shape, bf16),
            pltpu.SemaphoreType.DMA((3,)),
        ],
        compiler_params=pltpu.CompilerParams(vmem_limit_bytes=56 << 20),
        name="experts",
    )(slot, gates, rows, w_gate, w_up, w_down)


def local(
    hidden, gain_attn, w_query, w_key, w_value, w_out, gain_moe, expert_ids, expert_gates,
    w_gate, w_up, w_down, seg_lengths, slot_page,
):
    tok_rows = hidden.shape[0]
    shard_count = lax.axis_size("seq")
    shard_index = lax.axis_index("seq")
    half_dim = HEAD_DIM // 2
    inverse = rope_base ** (-2.0 * jnp.arange(half_dim, dtype=f32) / HEAD_DIM)
    inverse = jnp.concatenate([inverse, inverse])[None, :]
    gate_high = lax.reduce_precision(expert_gates, 8, 7)
    gate_low = expert_gates - gate_high
    blank = jnp.zeros((tok_rows, 2 * HEAD_DIM), f32)
    routing = jnp.concatenate(
        [expert_ids.astype(f32), gate_high, blank[:, : 16 - TOP], gate_low, blank[:, : HEAD_DIM - 16 - 2 * TOP]], axis=1
    )
    gathered, queries, first = front(
        seg_lengths, hidden, gain_attn[None, :], inverse, routing, w_query, w_key, w_value
    )
    gathered = gathered.reshape((shard_count,) + gathered.shape[3:])
    slot_count = slot_page.shape[0] // shard_count
    own_slots = lax.dynamic_slice_in_dim(slot_page, shard_index * slot_count, slot_count)
    terms, kv_cache, slot, gates = attend(
        shard_index, own_slots, queries, first, gathered, w_out, w_gate.shape[0]
    )
    rows, mid = row_gather(terms, hidden, gain_moe[None, :])
    made = experts(slot, gates, rows, w_gate, w_up, w_down)
    return (row_sum(made, mid), kv_cache)


def solution(mesh):
    placed = (
        P("seq", None),
        P(),
        P(None, "tp"),
        P(None, "tp"),
        P(None, "tp"),
        P("tp", None),
        P(),
        P("seq", None),
        P("seq", None),
        P("seq", None, "tp"),
        P("seq", None, "tp"),
        P("seq", "tp", None),
        P(),
        P(),
    )
    return jax.shard_map(
        local,
        mesh=mesh,
        in_specs=placed,
        out_specs=(P("seq", "tp"), P("seq", None, "tp")),
        check_vma=False,
    )
```

```python
import functools

import jax
import jax.numpy as jnp
import numpy as np
from jax import lax
from jax.experimental import pallas as pl
from jax.experimental.pallas import tpu as pltpu
from jax.sharding import PartitionSpec as P

HEAD_DIM = 128
TOP = 6
PAGE = 16
CAP = 24
RING = 4
MESH = pl.DeviceIdType.MESH
ANY = pl.BlockSpec(memory_space=pl.ANY)
WHOLE = pl.BlockSpec(memory_space=pltpu.VMEM)
epsilon = 1e-05
rope_base = 500000.0
masked_score = -1e30
bf16 = jnp.bfloat16
f32 = jnp.float32


def my_place():
    index = lax.axis_index("seq")
    return {
        "x": index // 8,
        "z": lax.rem(index // 2, RING),
        "c": lax.rem(index, 2),
        "y": lax.axis_index("tp"),
    }


def device_at(place):
    return ((place["x"] * RING + place["z"]) * 2 + place["c"], place["y"])


def moved(place, axis, step):
    size = 2 if axis == "c" else RING
    other = dict(place)
    other[axis] = lax.rem(place[axis] + step + size, size)
    return other


def enter(places):
    barrier = pltpu.get_barrier_semaphore()
    for place in places:
        pl.semaphore_signal(barrier, inc=1, device_id=device_at(place), device_id_type=MESH)
    pl.semaphore_wait(barrier, len(places))


class Links:
    def __init__(self, send_sem, recv_sem):
        self.send_sem, self.recv_sem, self.count = send_sem, recv_sem, 0
        self.started = []

    def push(self, src, dst, place):
        copy = pltpu.make_async_remote_copy(
            src_ref=src,
            dst_ref=dst,
            send_sem=self.send_sem.at[self.count],
            recv_sem=self.recv_sem.at[self.count],
            device_id=device_at(place),
            device_id_type=MESH,
        )
        self.count += 1
        copy.start()
        self.started.append(copy)
        return copy

    def finish(self):
        for copy in self.started:
            copy.wait_send()


def torus_gather(me, dims, parts, src, out, links, local_sem, beside):
    sibling = moved(me, "c", 1)

    def at(where, row0, rows):
        return out.at[tuple(where[d] for d in dims) + (pl.ds(row0, rows), slice(None))]

    own = {d: me[d] for d in dims}
    local = pltpu.make_async_copy(src, at(own, 0, src.shape[0]), local_sem)
    local.start()
    to_sibling = []
    for phase in range(len(parts[0][2])):
        if phase == 1:
            local.wait()
        live = []
        for row0, rows, order in parts:
            axis = order[phase]
            base = dict(own)
            for done in order[:phase]:
                base[done] = slice(None)
            whole = at(base, row0, rows)
            source = src.at[pl.ds(row0, rows), :] if phase == 0 else whole
            for step in (1, -1, 2):
                live.append((row0, rows, axis, base, step, links.push(source, whole, moved(me, axis, step))))
        if phase == 0:
            to_sibling.append(links.push(src, at(own, 0, src.shape[0]), sibling))
            beside()
        for row0, rows, axis, base, step, copy in live:
            copy.wait_recv()
            there = at({**base, axis: moved(me, axis, -step)[axis]}, row0, rows)
            to_sibling.append(links.push(there, there, sibling))
    for copy in to_sibling:
        copy.wait_recv()


def copies_of_gather(parts):
    return 1 + len(parts[0][2]) * len(parts) * 6


KV_PARTS = ((0, 80, ("x", "z")), (80, 64, ("z", "x")))
UNIT = (16, 128)
ROW_PARTS = (
    (0, 14, ("z", "y", "x")),
    (14, 13, ("y", "x", "z")),
    (27, 13, ("x", "z", "y")),
)
STREAMS = ((0, 1), (1, -1), (-1, 1), (2, -1))


def wave(stages):
    for stage in range(stages):
        for n in range(len(STREAMS)):
            yield stage, n


def to_units(values):
    rows, cols = values.shape
    return [
        values[:, j * 128 : (j + 1) * 128].reshape(rows // 16, 16, 128) for j in range(cols // 128)
    ]


def from_units(units, rows):
    group = rows // 16
    tiles = [units[j * group : (j + 1) * group].reshape(rows, 128) for j in range(units.shape[0] // group)]
    return jnp.concatenate(tiles, axis=1)


def stream_gather(me, src, out, links, local_sem):
    sibling = moved(me, "c", 1)

    def at(where, first, count):
        return out.at[where["x"], where["z"], where["c"], where["y"], pl.ds(first, count)]

    local = pltpu.make_async_copy(src, at(me, 0, src.shape[0]), local_sem)
    local.start()
    echo = []
    landed = {}
    for p, (u0, n, order) in enumerate(ROW_PARTS):
        piece = src.at[pl.ds(u0, n)]
        for step in (1, -1, 2):
            landed[p, step] = links.push(piece, at(me, u0, n), moved(me, order[0], step))
    state = {}

    def region(p, stream, ring, step):
        u0, n, order = ROW_PARTS[p]
        where = dict(me)
        where[order[0]] = moved(me, order[0], STREAMS[stream][0])[order[0]]
        if ring == 2:
            where[order[1]] = slice(None)
        where[order[ring]] = moved(me, order[ring], step)[order[ring]]
        return at(where, u0, n)

    def relay(ref):
        echo.append(links.push(ref, ref, sibling))

    for stage, stream in wave(6):
        step, way = STREAMS[stream]
        for p, (u0, n, order) in enumerate(ROW_PARTS):
            ring = 1 + stage // 3
            axis = order[ring]
            if stage % 3 == 0:
                if stage == 0:
                    if step == 0:
                        if p == 0:
                            local.wait()
                    else:
                        landed[p, -step if step != 2 else 2].wait_recv()
                else:
                    state[p, stream, 1, "far"].wait_recv()
                    whole = dict(me)
                    whole[order[0]] = moved(me, order[0], step)[order[0]]
                    whole[order[1]] = slice(None)
                    relay(at(whole, u0, n))
                own = region(p, stream, ring, 0)
                for w in (1, -1):
                    state[p, stream, ring, w] = links.push(own, own, moved(me, axis, w))
            elif stage % 3 == 1:
                state[p, stream, ring, way].wait_recv()
                near = region(p, stream, ring, -way)
                state[p, stream, ring, "far"] = links.push(near, near, moved(me, axis, way))
                state[p, stream, ring, -way].wait_recv()
                if ring == 2:
                    relay(near)
                    relay(region(p, stream, ring, way))
            elif ring == 2:
                state[p, stream, ring, "far"].wait_recv()
                relay(region(p, stream, ring, 2))
    for copy in echo:
        copy.wait_recv()


STREAM_COPIES = len(ROW_PARTS) * (3 + 4 * (3 + 4 + 3))


def turn(one, cosine, sine):
    return one * cosine + pltpu.roll(one, HEAD_DIM // 2, 1) * sine


def flat_gain(gain, first, count):
    return jnp.concatenate([gain[pl.ds(first + j, 1), :] for j in range(count)], axis=1)


def front_kernel(
    lengths, hidden, gain, inverse, expert_ids, expert_gates, w_query, w_key, w_value,
    gathered, queries, first, sent, wq, wk, wv, normed, send_sem, recv_sem, local_sem,
):
    me = my_place()
    loads = [
        pltpu.make_async_copy(src, dst, local_sem.at[1 + n])
        for n, (src, dst) in enumerate(((w_key, wk), (w_value, wv), (w_query, wq)))
    ]
    for load in loads:
        load.start()
    rows = hidden.shape[0]
    block = (me["x"] * RING + me["z"]) * 2 + me["c"]
    at = block * rows + lax.broadcasted_iota(jnp.int32, (rows, 1), 0)
    begin = jnp.zeros((rows, 1), jnp.int32)
    running = lengths[0]
    for n in range(1, lengths.shape[0]):
        begin = jnp.where(at >= running, running, begin)
        running = running + lengths[n]
    first[...] = begin
    angles = (at - begin).astype(f32) * inverse[...]
    cosine = jnp.cos(angles)
    lane = lax.broadcasted_iota(jnp.int32, angles.shape, 1)
    sine = jnp.where(lane < HEAD_DIM // 2, -jnp.sin(angles), jnp.sin(angles))
    wide = hidden[...].astype(f32)
    factor = lax.rsqrt(jnp.mean(wide * wide, axis=1, keepdims=True) + epsilon)
    normed[...] = (wide * factor * flat_gain(gain, 0, gain.shape[0])).astype(bf16)
    high = expert_gates[...].astype(bf16)
    low = (expert_gates[...] - high.astype(f32)).astype(bf16)
    to_at = lax.broadcasted_iota(jnp.int32, (16, TOP), 0)
    from_at = lax.broadcasted_iota(jnp.int32, (16, TOP), 1)
    top = (from_at == to_at).astype(f32).astype(bf16)
    below = (from_at + 8 == to_at).astype(f32).astype(bf16)

    def placed(where, values):
        return jnp.dot(where, values, preferred_element_type=f32)

    listed = placed(top, expert_ids[...].astype(f32).astype(bf16)) + placed(below, high)
    sent[rows : rows + 16, :HEAD_DIM] = listed.astype(bf16)
    sent[rows : rows + 16, HEAD_DIM:] = placed(below, low).astype(bf16)
    loads[0].wait()
    key = jnp.dot(normed[...], wk[...], preferred_element_type=f32)
    sent[:rows, :HEAD_DIM] = turn(key, cosine, sine).astype(bf16)
    loads[1].wait()
    sent[:rows, HEAD_DIM:] = jnp.dot(normed[...], wv[...], preferred_element_type=f32).astype(bf16)
    enter([moved(me, a, s) for a in ("x", "z") for s in (1, -1, 2)] + [moved(me, "c", 1)])
    links = Links(send_sem, recv_sem)

    def beside():
        loads[2].wait()
        raw = jnp.dot(normed[...], wq[...], preferred_element_type=f32)
        for head in range(raw.shape[1] // HEAD_DIM):
            cols = slice(head * HEAD_DIM, (head + 1) * HEAD_DIM)
            queries[:, cols] = turn(raw[:, cols], cosine, sine).astype(bf16)

    torus_gather(me, ("x", "z", "c"), KV_PARTS, sent, gathered, links, local_sem.at[0], beside)
    links.finish()


def front(lengths, hidden, gain, inverse, expert_ids, expert_gates, w_query, w_key, w_value):
    n = copies_of_gather(KV_PARTS)
    rows = hidden.shape[0]
    width = w_key.shape[1] + w_value.shape[1]
    return pl.pallas_call(
        front_kernel,
        out_shape=(
            jax.ShapeDtypeStruct((RING, RING, 2, rows + 16, width), bf16),
            jax.ShapeDtypeStruct((rows, w_query.shape[1]), bf16),
            jax.ShapeDtypeStruct((rows, 1), jnp.int32),
        ),
        in_specs=[pl.BlockSpec(memory_space=pltpu.SMEM)] + [WHOLE] * 5 + [ANY] * 3,
        out_specs=(ANY, WHOLE, WHOLE),
        scratch_shapes=[
            pltpu.VMEM((rows + 16, width), bf16),
            pltpu.VMEM(w_query.shape, bf16),
            pltpu.VMEM(w_key.shape, bf16),
            pltpu.VMEM(w_value.shape, bf16),
            pltpu.VMEM(hidden.shape, bf16),
            pltpu.SemaphoreType.DMA((n,)),
            pltpu.SemaphoreType.DMA((n,)),
            pltpu.SemaphoreType.DMA((4,)),
        ],
        compiler_params=pltpu.CompilerParams(
            collective_id=1, has_side_effects=True, vmem_limit_bytes=58 << 20
        ),
        name="front",
    )(lengths, hidden, gain, inverse, expert_ids, expert_gates, w_query, w_key, w_value)


def row_gather_kernel(
    terms, hidden, gain, out, mid, heard, squares, mid_v, row_v, send_sem, recv_sem, local_sem
):
    me = my_place()
    width = mid.shape[1]
    mine = pl.ds(pl.multiple_of(me["y"] * width, 128), width)
    peers = [moved(me, "y", s) for s in (1, 2, 3)]
    enter([moved(me, a, s) for a in ("x", "z") for s in (1, -1, 2)] + [moved(me, "c", 1)] + peers)
    links = Links(send_sem, recv_sem)
    sent = [
        links.push(terms.at[peer["y"]], heard.at[n], peer) for n, peer in enumerate(peers)
    ]
    total = terms[me["y"]].astype(f32)
    for n in range(3):
        sent[n].wait_recv()
        total = total + heard[n].astype(f32)
    mid_now = (hidden[:, mine].astype(f32) + total).astype(bf16)
    mid_v[...] = mid_now
    wide = mid_now.astype(f32)
    ours = jnp.sum(wide * wide, axis=1, keepdims=True)
    squares[3] = jnp.broadcast_to(ours, (ours.shape[0], 128)).T[:8]
    told = [links.push(squares.at[3], squares.at[n], peer) for n, peer in enumerate(peers)]
    whole = squares[3]
    for n in range(3):
        told[n].wait_recv()
        whole = whole + squares[n]
    whole = jnp.broadcast_to(whole[:1], (128, 128)).T[:, :1]
    factor = lax.rsqrt(whole * (1.0 / (RING * wide.shape[1])) + epsilon)
    ready = (wide * factor * flat_gain(gain, me["y"] * (width // 128), width // 128)).astype(bf16)
    for j, tile in enumerate(to_units(ready)):
        row_v[j * tile.shape[0] : (j + 1) * tile.shape[0]] = tile
    keep = pltpu.make_async_copy(mid_v, mid, local_sem.at[1])
    keep.start()
    stream_gather(me, row_v, out, links, local_sem.at[0])
    keep.wait()
    links.finish()


def row_gather(terms, hidden, gain):
    n = 6 + STREAM_COPIES
    rows, cols = terms.shape[1:]
    units = rows * cols // (UNIT[0] * UNIT[1])
    return pl.pallas_call(
        row_gather_kernel,
        out_shape=(
            jax.ShapeDtypeStruct((RING, RING, 2, RING, units) + UNIT, bf16),
            jax.ShapeDtypeStruct((rows, cols), bf16),
        ),
        in_specs=[WHOLE, WHOLE, WHOLE],
        out_specs=(ANY, ANY),
        scratch_shapes=[
            pltpu.VMEM((3, rows, cols), bf16),
            pltpu.VMEM((4, 8, rows), f32),
            pltpu.VMEM((rows, cols), bf16),
            pltpu.VMEM((units,) + UNIT, bf16),
            pltpu.SemaphoreType.DMA((n,)),
            pltpu.SemaphoreType.DMA((n,)),
            pltpu.SemaphoreType.DMA((2,)),
        ],
        compiler_params=pltpu.CompilerParams(
            collective_id=2, has_side_effects=True, vmem_limit_bytes=48 << 20
        ),
        name="row_gather",
    )(terms, hidden, gain)


SUM_DIMS = ("x", "z", "y")
SUM_STREAMS = ((2, 1), (1, -1), (-1, 1), (0, -1))


def row_sum_kernel(terms, mid, out, total, other, bufs, out_v, send_sem, recv_sem, local_sem):
    me = my_place()
    sibling = moved(me, "c", 1)
    enter([moved(me, a, s) for a in ("x", "z", "y") for s in (1, -1, 2)] + [sibling])
    links = Links(send_sem, recv_sem)

    def held(ref, where, u0, n):
        return ref.at[tuple(where[d] for d in SUM_DIMS) + (pl.ds(u0, n),)]

    def place(p, stream, **free):
        order = ROW_PARTS[p][2]
        where = dict(me)
        where[order[0]] = moved(me, order[0], SUM_STREAMS[stream][0])[order[0]]
        where.update(free)
        return where

    first = {}
    for stream in range(4):
        for p, (u0, n, order) in enumerate(ROW_PARTS):
            where = place(p, stream, **{order[1]: slice(None), order[2]: slice(None)})
            slot = stream * 3 + p
            keep = pltpu.make_async_copy(
                terms.at[where["x"], where["z"], me["c"], where["y"], pl.ds(u0, n)],
                held(total, where, u0, n),
                local_sem.at[slot],
            )
            keep.start()
            push = links.push(
                terms.at[where["x"], where["z"], sibling["c"], where["y"], pl.ds(u0, n)],
                held(other, where, u0, n),
                sibling,
            )
            first[p, stream] = (keep, push)

    def add(where, u0, n, buf, lead):
        span = pl.ds(u0, n)
        if lead is None:
            index = tuple(where[d] for d in SUM_DIMS) + (span,)
            total[index] = total[index] + buf[...]
            return

        def one(k, carry):
            index = tuple(k if d == lead else where[d] for d in SUM_DIMS) + (span,)
            total[index] = total[index] + buf[k]
            return carry

        lax.fori_loop(0, RING, one, 0)

    state = {}
    for stage, stream in wave(6):
        step, way = SUM_STREAMS[stream]
        for p, (u0, n, order) in enumerate(ROW_PARTS):
            if stage == 0:
                keep, push = first[p, stream]
                keep.wait()
                push.wait_recv()
                where = place(p, stream)
                span = pl.ds(u0, n)

                def one(k, carry, where=where, span=span, order=order):
                    spot = {order[1]: k // RING, order[2]: lax.rem(k, RING)}
                    index = tuple(spot.get(d, where[d]) for d in SUM_DIMS) + (span,)
                    total[index] = total[index] + other[index]
                    return carry

                lax.fori_loop(0, RING * RING, one, 0)
            ring = 2 - stage // 3
            axis = order[ring]
            lead = order[1] if ring == 2 else None
            free = {order[1]: slice(None)} if ring == 2 else {}
            far, near, back = bufs[((2 - ring) * 4 + stream) * 3 + p]
            at = lambda s: place(p, stream, **free, **{axis: moved(me, axis, s)[axis]})
            if stage % 3 == 0:
                state[p, stream, ring, "far"] = links.push(held(total, at(2), u0, n), far, moved(me, axis, way))
                state[p, stream, ring, "back"] = links.push(held(total, at(-way), u0, n), back, moved(me, axis, -way))
            elif stage % 3 == 1:
                state[p, stream, ring, "far"].wait_recv()
                add(at(way), u0, n, far, lead)
                state[p, stream, ring, "near"] = links.push(held(total, at(way), u0, n), near, moved(me, axis, way))
            else:
                state[p, stream, ring, "back"].wait_recv()
                add(at(0), u0, n, back, lead)
                state[p, stream, ring, "near"].wait_recv()
                add(at(0), u0, n, near, lead)
                if ring == 1 and step != 0:
                    state[p, stream, "last"] = links.push(
                        held(total, place(p, stream), u0, n), bufs[24 + stream * 3 + p][0], moved(me, order[0], step)
                    )
    for stream in range(3):
        for p, (u0, n, order) in enumerate(ROW_PARTS):
            state[p, stream, "last"].wait_recv()
            add(me, u0, n, bufs[24 + stream * 3 + p][0], None)
    done = from_units(total[me["x"], me["z"], me["y"]], out.shape[0])
    out_v[...] = (mid[...].astype(f32) + done.astype(f32)).astype(bf16)
    write = pltpu.make_async_copy(out_v, out, local_sem.at[12])
    write.start()
    write.wait()
    links.finish()


def row_sum(terms, mid):
    rows, cols = mid.shape
    units = terms.shape[4]
    n = 12 + 3 * (4 * 6 + 3)
    bufs = []
    for ring in (2, 1):
        for stream in range(4):
            for _, count, _ in ROW_PARTS:
                bufs += [((RING,) if ring == 2 else ()) + (count,) + UNIT] * 3
    for stream in range(3):
        for _, count, _ in ROW_PARTS:
            bufs += [(count,) + UNIT]

    def kernel(terms, mid, out, total, other, *rest):
        flat, rest = rest[: len(bufs)], rest[len(bufs) :]
        sets = [flat[3 * k : 3 * k + 3] for k in range(24)] + [flat[72 + k : 73 + k] for k in range(9)]
        row_sum_kernel(terms, mid, out, total, other, sets, *rest)

    return pl.pallas_call(
        kernel,
        out_shape=jax.ShapeDtypeStruct((rows, cols), bf16),
        in_specs=[ANY, WHOLE],
        out_specs=ANY,
        scratch_shapes=[
            pltpu.VMEM((RING, RING, RING, units) + UNIT, bf16),
            pltpu.VMEM((RING, RING, RING, units) + UNIT, bf16),
        ]
        + [pltpu.VMEM(shape, bf16) for shape in bufs]
        + [
            pltpu.VMEM((rows, cols), bf16),
            pltpu.SemaphoreType.DMA((n,)),
            pltpu.SemaphoreType.DMA((n,)),
            pltpu.SemaphoreType.DMA((13,)),
        ],
        compiler_params=pltpu.CompilerParams(
            collective_id=3, has_side_effects=True, vmem_limit_bytes=48 << 20
        ),
        name="row_sum",
    )(terms, mid)


def attend_kernel(
    where, pages, queries, first, gathered, w_out, terms, cache, slot, gates,
    full, wo, zeros, attended, sems, page_sems,
):
    span = min(9, full.shape[0])
    block, start = where[0], where[1]
    slots = cache.shape[0]
    rows = queries.shape[0]
    grab = pltpu.make_async_copy(gathered, full, sems.at[0])
    grab.start()
    load = pltpu.make_async_copy(w_out, wo, sems.at[1])
    load.start()
    zeros[...] = jnp.zeros_like(zeros)

    def page_copy(n, page):
        return pltpu.make_async_copy(
            full.at[page // 8, pl.ds(pl.multiple_of(lax.rem(page, 8) * PAGE, PAGE), PAGE), :],
            cache.at[n],
            page_sems.at[n],
        )

    def empty_copy(n):
        return pltpu.make_async_copy(zeros, cache.at[n], page_sems.at[n])

    def send(n, carry):
        page = pages[n]

        @pl.when(page >= 0)
        def _():
            page_copy(n, page).start()

        @pl.when(page < 0)
        def _():
            empty_copy(n).start()

        return carry

    grab.wait()
    lax.fori_loop(0, slots, send, 0)
    width = span * rows
    held = full[pl.ds(start, span), :rows, :]
    keys = held[:, :, :HEAD_DIM].reshape(width, HEAD_DIM)
    values = held[:, :, HEAD_DIM:].reshape(width, HEAD_DIM)
    key_at = start * rows + lax.broadcasted_iota(jnp.int32, (rows, width), 1)
    query_at = block * rows + lax.broadcasted_iota(jnp.int32, (rows, width), 0)
    allowed = (key_at <= query_at) & (key_at >= first[...])
    for head in range(queries.shape[1] // HEAD_DIM):
        cols = pl.ds(head * HEAD_DIM, HEAD_DIM)
        scores = lax.dot_general(
            queries[:, cols], keys, (((1,), (1,)), ((), ())), preferred_element_type=f32
        ) * (HEAD_DIM**-0.5)
        scores = jnp.where(allowed, scores, masked_score)
        weights = jnp.where(allowed, jnp.exp(scores - jnp.max(scores, axis=1, keepdims=True)), 0.0)
        totals = jnp.sum(weights, axis=1, keepdims=True)
        mixed = jnp.dot(weights.astype(bf16), values, preferred_element_type=f32)
        attended[:, cols] = (mixed / totals).astype(bf16)
    load.wait()
    out_width = terms.shape[2]
    for half in range(2):
        cols = slice(2 * half * out_width, 2 * (half + 1) * out_width)
        part = jnp.dot(attended[...], wo[:, cols], preferred_element_type=f32).astype(bf16)
        terms[2 * half] = part[:, :out_width]
        terms[2 * half + 1] = part[:, out_width:]
    meta = full[:, rows : rows + 16, :]
    ids = meta[:, :TOP, :HEAD_DIM].astype(f32)
    weight = meta[:, 8 : 8 + TOP, :HEAD_DIM].astype(f32) + meta[:, 8 : 8 + TOP, HEAD_DIM:].astype(f32)
    blocks = meta.shape[0]
    earlier = lax.broadcasted_iota(jnp.int32, (rows, rows), 0) < lax.broadcasted_iota(jnp.int32, (rows, rows), 1)
    earlier = earlier.astype(f32).astype(bf16)
    odd = lax.rem(lax.broadcasted_iota(jnp.int32, (blocks, rows), 0), PAIR).astype(f32) * CAP
    n_exp = slot.shape[0]
    for e in range(n_exp):
        hits = ids == (block * n_exp + e).astype(f32)
        named = jnp.max(hits.astype(f32), axis=1)
        rank = jnp.dot(named.astype(bf16), earlier, preferred_element_type=f32)
        place = jnp.where(named > 0.0, rank + odd, -1.0)
        slot[e] = jnp.concatenate([place.reshape(blocks // PAIR, PAIR, rows)[:, b] for b in range(PAIR)], axis=1)
        share = jnp.sum(jnp.where(hits, weight, 0.0), axis=1)
        gates[e] = jnp.concatenate([share.reshape(blocks // PAIR, PAIR, rows)[:, b] for b in range(PAIR)], axis=1)

    def settle(n, carry):
        empty_copy(n).wait()
        return carry

    lax.fori_loop(0, slots, settle, 0)


def attend(block, pages, slots, queries, first, gathered, w_out, n_exp):
    blocks = gathered.shape[0]
    span = min(9, blocks)
    start = jnp.clip(block - 8, 0, blocks - span)
    width = gathered.shape[2]
    rows = queries.shape[0]
    terms = (RING, rows, w_out.shape[1] // RING)
    slot = (n_exp, blocks // PAIR, PAIR * rows)

    def whole(shape):
        return pl.BlockSpec(shape, lambda i, *_: (0,) * len(shape))

    return pl.pallas_call(
        attend_kernel,
        grid_spec=pltpu.PrefetchScalarGridSpec(
            num_scalar_prefetch=2,
            grid=(1,),
            in_specs=[whole(queries.shape), whole(first.shape), ANY, ANY],
            out_specs=(whole(terms), ANY, whole(slot), whole(slot)),
            scratch_shapes=[
                pltpu.VMEM(gathered.shape, bf16),
                pltpu.VMEM(w_out.shape, bf16),
                pltpu.VMEM((PAGE, width), bf16),
                pltpu.VMEM(queries.shape, bf16),
                pltpu.SemaphoreType.DMA((2,)),
                pltpu.SemaphoreType.DMA((slots,)),
            ],
        ),
        out_shape=(
            jax.ShapeDtypeStruct(terms, bf16),
            jax.ShapeDtypeStruct((slots, PAGE, width), bf16),
            jax.ShapeDtypeStruct(slot, f32),
            jax.ShapeDtypeStruct(slot, f32),
        ),
        compiler_params=pltpu.CompilerParams(vmem_limit_bytes=58 << 20),
        name="attend",
    )(jnp.stack([block, start]).astype(jnp.int32), pages, queries, first, gathered, w_out)


PAIR = 2


def expert_kernel(slot, gates, rows, w_gate, w_up, w_down, out, packed, scale, wgu, wd, sems):
    step = pl.program_id(0)
    groups = 8
    tokens = groups * UNIT[0]
    tiles = rows.shape[4] // groups
    quarter = tiles * UNIT[1]
    pair_cap = PAIR * CAP
    n_exp, _, ff = w_gate.shape
    loads = [
        pltpu.make_async_copy(src, dst, sems.at[n])
        for n, (src, dst) in enumerate(
            ((w_gate, wgu.at[:, :, pl.ds(0, ff)]), (w_up, wgu.at[:, :, pl.ds(ff, ff)]), (w_down, wd))
        )
    ]

    @pl.when(step == 0)
    def _():
        for load in loads:
            load.start()

    row = lax.broadcasted_iota(jnp.int32, (pair_cap, PAIR * tokens), 0).astype(f32)
    picks = []
    for z in range(RING):
        span = slice(z * pair_cap, (z + 1) * pair_cap)
        same = [
            jnp.broadcast_to(slot[e, pl.ds(step * RING + z, 1), :], row.shape) == row for e in range(n_exp)
        ]
        for e in range(n_exp):
            scale[e, span, :] = jnp.sum(
                jnp.where(same[e], gates[e, pl.ds(step * RING + z, 1), :], 0.0), axis=1, keepdims=True
            )
        picks.append(jnp.concatenate([m.astype(f32) for m in same], axis=0).astype(bf16))
        for h in range(2):
            parts = []
            for k in range(2):
                for j in range(tiles):
                    units = slice(j * groups, (j + 1) * groups)
                    parts.append(rows[0, z, :, 2 * h + k, units].reshape(PAIR * tokens, 128))
            got = jnp.dot(picks[z], jnp.concatenate(parts, axis=1), preferred_element_type=f32).astype(bf16)
            for e in range(n_exp):
                packed[e, span, 2 * h * quarter : 2 * (h + 1) * quarter] = got[e * pair_cap : (e + 1) * pair_cap]

    @pl.when(step == 0)
    def _():
        for load in loads:
            load.wait()

    for e in range(n_exp):
        both = jnp.dot(packed[e], wgu[e], preferred_element_type=f32)
        gate_term, up_term = both[:, :ff], both[:, ff:]
        act = (gate_term / (1.0 + jnp.exp(-gate_term)) * up_term).astype(bf16)
        for h in range(2):
            cols = slice(2 * h * quarter, 2 * (h + 1) * quarter)
            down = jnp.dot(act, wd[e, :, cols], preferred_element_type=f32)
            packed[e, :, cols] = (down * scale[e]).astype(bf16)
    for z in range(RING):
        span = slice(z * pair_cap, (z + 1) * pair_cap)
        for h in range(2):
            cols = slice(2 * h * quarter, 2 * (h + 1) * quarter)
            made = jnp.concatenate([packed[e, span, cols] for e in range(n_exp)], axis=0)
            back = lax.dot_general(picks[z], made, (((0,), (0,)), ((), ())), preferred_element_type=f32).astype(bf16)
            for k in range(2):
                for j in range(tiles):
                    n = k * tiles + j
                    out[0, z, :, 2 * h + k, j * groups : (j + 1) * groups] = back[:, n * 128 : (n + 1) * 128].reshape(
                        PAIR, groups, *UNIT
                    )


def experts(slot, gates, rows, w_gate, w_up, w_down):
    n_exp, width, ff = w_gate.shape
    taken = (n_exp, RING * PAIR * CAP)
    whole = pl.BlockSpec(slot.shape, lambda i: (0, 0, 0))
    some = pl.BlockSpec((1,) + rows.shape[1:], lambda i: (i,) + (0,) * (len(rows.shape) - 1))
    return pl.pallas_call(
        expert_kernel,
        grid=(RING,),
        in_specs=[whole, whole, some, ANY, ANY, ANY],
        out_specs=some,
        out_shape=jax.ShapeDtypeStruct(rows.shape, bf16),
        scratch_shapes=[
            pltpu.VMEM(taken + (width,), bf16),
            pltpu.VMEM(taken + (1,), f32),
            pltpu.VMEM((n_exp, width, 2 * ff), bf16),
            pltpu.VMEM(w_down.shape, bf16),
            pltpu.SemaphoreType.DMA((3,)),
        ],
        compiler_params=pltpu.CompilerParams(vmem_limit_bytes=56 << 20),
        name="experts",
    )(slot, gates, rows, w_gate, w_up, w_down)


def local(
    hidden, gain_attn, w_query, w_key, w_value, w_out, gain_moe, expert_ids, expert_gates,
    w_gate, w_up, w_down, seg_lengths, slot_page,
):
    shard_count = lax.axis_size("seq")
    shard_index = lax.axis_index("seq")
    steps = np.arange(HEAD_DIM, dtype=np.float32) % (HEAD_DIM // 2)
    inverse = jnp.asarray(np.float32(rope_base) ** (np.float32(-2.0) * steps / np.float32(HEAD_DIM)))[None, :]
    gathered, queries, first = front(
        seg_lengths, hidden, gain_attn.reshape(-1, 128), inverse, expert_ids.T, expert_gates.T, w_query, w_key, w_value
    )
    gathered = gathered.reshape((shard_count,) + gathered.shape[3:])
    slot_count = slot_page.shape[0] // shard_count
    own_slots = lax.dynamic_slice_in_dim(slot_page, shard_index * slot_count, slot_count)
    terms, kv_cache, slot, gates = attend(
        shard_index, own_slots, slot_count, queries, first, gathered, w_out, w_gate.shape[0]
    )
    rows, mid = row_gather(terms, hidden, gain_moe.reshape(-1, 128))
    made = experts(slot, gates, rows, w_gate, w_up, w_down)
    return (row_sum(made, mid), kv_cache)


def solution(mesh):
    placed = (
        P("seq", None),
        P(),
        P(None, "tp"),
        P(None, "tp"),
        P(None, "tp"),
        P("tp", None),
        P(),
        P("seq", None),
        P("seq", None),
        P("seq", None, "tp"),
        P("seq", None, "tp"),
        P("seq", "tp", None),
        P(),
        P(),
    )
    return jax.shard_map(
        local,
        mesh=mesh,
        in_specs=placed,
        out_specs=(P("seq", "tp"), P("seq", None, "tp")),
        check_vma=False,
    )
```

```python
import functools

import jax
import jax.numpy as jnp
import numpy as np
from jax import lax
from jax.experimental import pallas as pl
from jax.experimental.pallas import tpu as pltpu
from jax.sharding import PartitionSpec as P

HEAD_DIM = 128
TOP = 6
PAGE = 16
CAP = 24
RING = 4
MESH = pl.DeviceIdType.MESH
ANY = pl.BlockSpec(memory_space=pl.ANY)
WHOLE = pl.BlockSpec(memory_space=pltpu.VMEM)
epsilon = 1e-05
rope_base = 500000.0
masked_score = -1e30
bf16 = jnp.bfloat16
f32 = jnp.float32


def my_place():
    index = lax.axis_index("seq")
    return {
        "x": index // 8,
        "z": lax.rem(index // 2, RING),
        "c": lax.rem(index, 2),
        "y": lax.axis_index("tp"),
    }


def device_at(place):
    return ((place["x"] * RING + place["z"]) * 2 + place["c"], place["y"])


def moved(place, axis, step):
    size = 2 if axis == "c" else RING
    other = dict(place)
    other[axis] = lax.rem(place[axis] + step + size, size)
    return other


def enter(places):
    barrier = pltpu.get_barrier_semaphore()
    for place in places:
        pl.semaphore_signal(barrier, inc=1, device_id=device_at(place), device_id_type=MESH)
    pl.semaphore_wait(barrier, len(places))


class Links:
    def __init__(self, send_sem, recv_sem):
        self.send_sem, self.recv_sem, self.count = send_sem, recv_sem, 0
        self.started = []

    def push(self, src, dst, place):
        copy = pltpu.make_async_remote_copy(
            src_ref=src,
            dst_ref=dst,
            send_sem=self.send_sem.at[self.count],
            recv_sem=self.recv_sem.at[self.count],
            device_id=device_at(place),
            device_id_type=MESH,
        )
        self.count += 1
        copy.start()
        self.started.append(copy)
        return copy

    def finish(self):
        for copy in self.started:
            copy.wait_send()


def torus_gather(me, dims, parts, src, out, links, local_sem, beside):
    sibling = moved(me, "c", 1)

    def at(where, row0, rows):
        return out.at[tuple(where[d] for d in dims) + (pl.ds(row0, rows), slice(None))]

    own = {d: me[d] for d in dims}
    local = pltpu.make_async_copy(src, at(own, 0, src.shape[0]), local_sem)
    local.start()
    to_sibling = []
    for phase in range(len(parts[0][2])):
        if phase == 1:
            local.wait()
        live = []
        for row0, rows, order in parts:
            axis = order[phase]
            base = dict(own)
            for done in order[:phase]:
                base[done] = slice(None)
            whole = at(base, row0, rows)
            source = src.at[pl.ds(row0, rows), :] if phase == 0 else whole
            for step in (1, -1, 2):
                live.append((row0, rows, axis, base, step, links.push(source, whole, moved(me, axis, step))))
        if phase == 0:
            to_sibling.append(links.push(src, at(own, 0, src.shape[0]), sibling))
            beside()
        for row0, rows, axis, base, step, copy in live:
            copy.wait_recv()
            there = at({**base, axis: moved(me, axis, -step)[axis]}, row0, rows)
            to_sibling.append(links.push(there, there, sibling))
    for copy in to_sibling:
        copy.wait_recv()


def copies_of_gather(parts):
    return 1 + len(parts[0][2]) * len(parts) * 6


KV_PARTS = ((0, 80, ("x", "z")), (80, 64, ("z", "x")))
UNIT = (16, 128)
ROW_PARTS = (
    (0, 14, ("z", "y", "x")),
    (14, 13, ("y", "x", "z")),
    (27, 13, ("x", "z", "y")),
)
STREAMS = ((0, 1), (1, -1), (-1, 1), (2, -1))


def wave(stages):
    for stage in range(stages):
        for n in range(len(STREAMS)):
            yield stage, n


def to_units(values):
    rows, cols = values.shape
    return [
        values[:, j * 128 : (j + 1) * 128].reshape(rows // 16, 16, 128) for j in range(cols // 128)
    ]


def from_units(units, rows):
    group = rows // 16
    tiles = [units[j * group : (j + 1) * group].reshape(rows, 128) for j in range(units.shape[0] // group)]
    return jnp.concatenate(tiles, axis=1)


def stream_gather(me, src, out, links, local_sem):
    sibling = moved(me, "c", 1)

    def at(where, first, count):
        return out.at[where["x"], where["z"], where["c"], where["y"], pl.ds(first, count)]

    local = pltpu.make_async_copy(src, at(me, 0, src.shape[0]), local_sem)
    local.start()
    echo = []
    landed = {}
    for p, (u0, n, order) in enumerate(ROW_PARTS):
        piece = src.at[pl.ds(u0, n)]
        for step in (1, -1, 2):
            landed[p, step] = links.push(piece, at(me, u0, n), moved(me, order[0], step))
    state = {}

    def region(p, stream, ring, step):
        u0, n, order = ROW_PARTS[p]
        where = dict(me)
        where[order[0]] = moved(me, order[0], STREAMS[stream][0])[order[0]]
        if ring == 2:
            where[order[1]] = slice(None)
        where[order[ring]] = moved(me, order[ring], step)[order[ring]]
        return at(where, u0, n)

    def relay(ref):
        echo.append(links.push(ref, ref, sibling))

    for stage, stream in wave(6):
        step, way = STREAMS[stream]
        for p, (u0, n, order) in enumerate(ROW_PARTS):
            ring = 1 + stage // 3
            axis = order[ring]
            if stage % 3 == 0:
                if stage == 0:
                    if step == 0:
                        if p == 0:
                            local.wait()
                    else:
                        landed[p, -step if step != 2 else 2].wait_recv()
                else:
                    state[p, stream, 1, "far"].wait_recv()
                    whole = dict(me)
                    whole[order[0]] = moved(me, order[0], step)[order[0]]
                    whole[order[1]] = slice(None)
                    relay(at(whole, u0, n))
                own = region(p, stream, ring, 0)
                for w in (1, -1):
                    state[p, stream, ring, w] = links.push(own, own, moved(me, axis, w))
            elif stage % 3 == 1:
                state[p, stream, ring, way].wait_recv()
                near = region(p, stream, ring, -way)
                state[p, stream, ring, "far"] = links.push(near, near, moved(me, axis, way))
                state[p, stream, ring, -way].wait_recv()
                if ring == 2:
                    relay(near)
                    relay(region(p, stream, ring, way))
            elif ring == 2:
                state[p, stream, ring, "far"].wait_recv()
                relay(region(p, stream, ring, 2))
    for copy in echo:
        copy.wait_recv()


STREAM_COPIES = len(ROW_PARTS) * (3 + 4 * (3 + 4 + 3))


def turn(one, cosine, sine):
    return one * cosine + pltpu.roll(one, HEAD_DIM // 2, 1) * sine


def flat_gain(gain, first, count):
    return jnp.concatenate([gain[pl.ds(first + j, 1), :] for j in range(count)], axis=1)


def front_kernel(
    lengths, hidden, gain, inverse, expert_ids, expert_gates, w_query, w_key, w_value,
    gathered, queries, first, sent, wq, wk, wv, normed, send_sem, recv_sem, local_sem,
):
    me = my_place()
    loads = [
        pltpu.make_async_copy(src, dst, local_sem.at[1 + n])
        for n, (src, dst) in enumerate(((w_key, wk), (w_value, wv), (w_query, wq)))
    ]
    for load in loads:
        load.start()
    rows = hidden.shape[0]
    block = (me["x"] * RING + me["z"]) * 2 + me["c"]
    at = block * rows + lax.broadcasted_iota(jnp.int32, (rows, 1), 0)
    begin = jnp.zeros((rows, 1), jnp.int32)
    running = lengths[0]
    for n in range(1, lengths.shape[0]):
        begin = jnp.where(at >= running, running, begin)
        running = running + lengths[n]
    first[...] = begin
    angles = (at - begin).astype(f32) * inverse[...]
    cosine = jnp.cos(angles)
    lane = lax.broadcasted_iota(jnp.int32, angles.shape, 1)
    sine = jnp.where(lane < HEAD_DIM // 2, -jnp.sin(angles), jnp.sin(angles))
    wide = hidden[...].astype(f32)
    factor = lax.rsqrt(jnp.mean(wide * wide, axis=1, keepdims=True) + epsilon)
    normed[...] = (wide * factor * flat_gain(gain, 0, gain.shape[0])).astype(bf16)
    high = expert_gates[...].astype(bf16)
    low = (expert_gates[...] - high.astype(f32)).astype(bf16)
    to_at = lax.broadcasted_iota(jnp.int32, (16, TOP), 0)
    from_at = lax.broadcasted_iota(jnp.int32, (16, TOP), 1)
    top = (from_at == to_at).astype(f32).astype(bf16)
    below = (from_at + 8 == to_at).astype(f32).astype(bf16)

    def placed(where, values):
        return jnp.dot(where, values, preferred_element_type=f32)

    listed = placed(top, expert_ids[...].astype(f32).astype(bf16)) + placed(below, high)
    sent[rows : rows + 16, :HEAD_DIM] = listed.astype(bf16)
    sent[rows : rows + 16, HEAD_DIM:] = placed(below, low).astype(bf16)
    loads[0].wait()
    key = jnp.dot(normed[...], wk[...], preferred_element_type=f32)
    sent[:rows, :HEAD_DIM] = turn(key, cosine, sine).astype(bf16)
    loads[1].wait()
    sent[:rows, HEAD_DIM:] = jnp.dot(normed[...], wv[...], preferred_element_type=f32).astype(bf16)
    enter([moved(me, a, s) for a in ("x", "z") for s in (1, -1, 2)] + [moved(me, "c", 1)])
    links = Links(send_sem, recv_sem)

    def beside():
        loads[2].wait()
        raw = jnp.dot(normed[...], wq[...], preferred_element_type=f32)
        for head in range(raw.shape[1] // HEAD_DIM):
            cols = slice(head * HEAD_DIM, (head + 1) * HEAD_DIM)
            queries[:, cols] = turn(raw[:, cols], cosine, sine).astype(bf16)

    torus_gather(me, ("x", "z", "c"), KV_PARTS, sent, gathered, links, local_sem.at[0], beside)
    links.finish()


def front(lengths, hidden, gain, inverse, expert_ids, expert_gates, w_query, w_key, w_value):
    n = copies_of_gather(KV_PARTS)
    rows = hidden.shape[0]
    width = w_key.shape[1] + w_value.shape[1]
    return pl.pallas_call(
        front_kernel,
        out_shape=(
            jax.ShapeDtypeStruct((RING, RING, 2, rows + 16, width), bf16),
            jax.ShapeDtypeStruct((rows, w_query.shape[1]), bf16),
            jax.ShapeDtypeStruct((rows, 1), jnp.int32),
        ),
        in_specs=[pl.BlockSpec(memory_space=pltpu.SMEM)] + [WHOLE] * 5 + [ANY] * 3,
        out_specs=(ANY, WHOLE, WHOLE),
        scratch_shapes=[
            pltpu.VMEM((rows + 16, width), bf16),
            pltpu.VMEM(w_query.shape, bf16),
            pltpu.VMEM(w_key.shape, bf16),
            pltpu.VMEM(w_value.shape, bf16),
            pltpu.VMEM(hidden.shape, bf16),
            pltpu.SemaphoreType.DMA((n,)),
            pltpu.SemaphoreType.DMA((n,)),
            pltpu.SemaphoreType.DMA((4,)),
        ],
        compiler_params=pltpu.CompilerParams(
            collective_id=1, has_side_effects=True, vmem_limit_bytes=58 << 20
        ),
        name="front",
    )(lengths, hidden, gain, inverse, expert_ids, expert_gates, w_query, w_key, w_value)


def row_gather_kernel(
    terms, hidden, gain, out, mid, heard, squares, mid_v, row_v, send_sem, recv_sem, local_sem
):
    me = my_place()
    width = mid.shape[1]
    mine = pl.ds(pl.multiple_of(me["y"] * width, 128), width)
    peers = [moved(me, "y", s) for s in (1, 2, 3)]
    enter([moved(me, a, s) for a in ("x", "z") for s in (1, -1, 2)] + [moved(me, "c", 1)] + peers)
    links = Links(send_sem, recv_sem)
    sent = [
        links.push(terms.at[peer["y"]], heard.at[n], peer) for n, peer in enumerate(peers)
    ]
    total = terms[me["y"]].astype(f32)
    for n in range(3):
        sent[n].wait_recv()
        total = total + heard[n].astype(f32)
    mid_now = (hidden[:, mine].astype(f32) + total).astype(bf16)
    mid_v[...] = mid_now
    wide = mid_now.astype(f32)
    ours = jnp.sum(wide * wide, axis=1, keepdims=True)
    squares[3] = jnp.broadcast_to(ours, (ours.shape[0], 128)).T[:8]
    told = [links.push(squares.at[3], squares.at[n], peer) for n, peer in enumerate(peers)]
    whole = squares[3]
    for n in range(3):
        told[n].wait_recv()
        whole = whole + squares[n]
    whole = jnp.broadcast_to(whole[:1], (128, 128)).T[:, :1]
    factor = lax.rsqrt(whole * (1.0 / (RING * wide.shape[1])) + epsilon)
    ready = (wide * factor * flat_gain(gain, me["y"] * (width // 128), width // 128)).astype(bf16)
    for j, tile in enumerate(to_units(ready)):
        row_v[j * tile.shape[0] : (j + 1) * tile.shape[0]] = tile
    keep = pltpu.make_async_copy(mid_v, mid, local_sem.at[1])
    keep.start()
    stream_gather(me, row_v, out, links, local_sem.at[0])
    keep.wait()
    links.finish()


def row_gather(terms, hidden, gain):
    n = 6 + STREAM_COPIES
    rows, cols = terms.shape[1:]
    units = rows * cols // (UNIT[0] * UNIT[1])
    return pl.pallas_call(
        row_gather_kernel,
        out_shape=(
            jax.ShapeDtypeStruct((RING, RING, 2, RING, units) + UNIT, bf16),
            jax.ShapeDtypeStruct((rows, cols), bf16),
        ),
        in_specs=[WHOLE, WHOLE, WHOLE],
        out_specs=(ANY, ANY),
        scratch_shapes=[
            pltpu.VMEM((3, rows, cols), bf16),
            pltpu.VMEM((4, 8, rows), f32),
            pltpu.VMEM((rows, cols), bf16),
            pltpu.VMEM((units,) + UNIT, bf16),
            pltpu.SemaphoreType.DMA((n,)),
            pltpu.SemaphoreType.DMA((n,)),
            pltpu.SemaphoreType.DMA((2,)),
        ],
        compiler_params=pltpu.CompilerParams(
            collective_id=2, has_side_effects=True, vmem_limit_bytes=48 << 20
        ),
        name="row_gather",
    )(terms, hidden, gain)


SUM_DIMS = ("x", "z", "y")
SUM_STREAMS = ((2, 1), (1, -1), (-1, 1), (0, -1))


def row_sum_kernel(slot, source, mid, out, terms, made, other, bufs, out_v, send_sem, recv_sem, local_sem, in_sems):
    me = my_place()
    takes = []
    for x in range(RING):
        rows = pl.ds(x * RING * PAIR * CAP, RING * PAIR * CAP)
        takes.append(pltpu.make_async_copy(source.at[:, rows, :], made.at[:, rows, :], in_sems.at[x]))
        takes[x].start()
    sibling = moved(me, "c", 1)
    enter([moved(me, a, s) for a in ("x", "z", "y") for s in (1, -1, 2)] + [sibling])
    links = Links(send_sem, recv_sem)

    groups = 8
    tokens = groups * UNIT[0]
    tiles = terms.shape[4] // groups
    pair_cap = PAIR * CAP
    n_exp, _, width = made.shape

    def spread(x, z):
        chip = x * RING + z
        at = pl.multiple_of(chip * pair_cap, 16)
        row = lax.broadcasted_iota(jnp.int32, (pair_cap, PAIR * tokens), 0).astype(f32)
        same = [jnp.broadcast_to(slot[e, pl.ds(chip, 1), :], row.shape) == row for e in range(n_exp)]
        pick = jnp.concatenate([m.astype(f32) for m in same], axis=0).astype(bf16)
        for h in range(2):
            cols = slice(h * width // 2, (h + 1) * width // 2)
            rows = jnp.concatenate([made[e, pl.ds(at, pair_cap), cols] for e in range(n_exp)], axis=0)
            back = lax.dot_general(pick, rows, (((0,), (0,)), ((), ())), preferred_element_type=f32).astype(bf16)
            for k in range(2):
                for j in range(tiles):
                    n = k * tiles + j
                    terms[x, z, :, 2 * h + k, j * groups : (j + 1) * groups] = back[:, n * 128 : (n + 1) * 128].reshape(
                        PAIR, groups, *UNIT
                    )

    def one_chip(chip, carry):
        spread(chip // RING, lax.rem(chip, RING))
        return carry

    for x in range(RING):
        takes[x].wait()
        lax.fori_loop(x * RING, (x + 1) * RING, one_chip, 0)

    def held(where, u0, n):
        return terms.at[where["x"], where["z"], me["c"], where["y"], pl.ds(u0, n)]

    def place(p, stream, **free):
        order = ROW_PARTS[p][2]
        where = dict(me)
        where[order[0]] = moved(me, order[0], SUM_STREAMS[stream][0])[order[0]]
        where.update(free)
        return where

    first = {}
    for stream in range(4):
        for p, (u0, n, order) in enumerate(ROW_PARTS):
            where = place(p, stream, **{order[1]: slice(None), order[2]: slice(None)})
            first[p, stream] = links.push(
                terms.at[where["x"], where["z"], sibling["c"], where["y"], pl.ds(u0, n)],
                other.at[where["x"], where["z"], where["y"], pl.ds(u0, n)],
                sibling,
            )

    def add(where, u0, n, buf, lead):
        span = pl.ds(u0, n)
        if lead is None:
            index = (where["x"], where["z"], me["c"], where["y"], span)
            terms[index] = terms[index] + buf[...]
            return

        def one(k, carry):
            spot = {**where, lead: k}
            index = (spot["x"], spot["z"], me["c"], spot["y"], span)
            terms[index] = terms[index] + buf[k]
            return carry

        lax.fori_loop(0, RING, one, 0)

    state = {}
    for stage, stream in wave(6):
        step, way = SUM_STREAMS[stream]
        for p, (u0, n, order) in enumerate(ROW_PARTS):
            if stage == 0:
                first[p, stream].wait_recv()
                where = place(p, stream)
                span = pl.ds(u0, n)

                def one(k, carry, where=where, span=span, order=order):
                    spot = {order[1]: k // RING, order[2]: lax.rem(k, RING)}
                    x, z, y = (spot.get(d, where[d]) for d in SUM_DIMS)
                    terms[x, z, me["c"], y, span] = terms[x, z, me["c"], y, span] + other[x, z, y, span]
                    return carry

                lax.fori_loop(0, RING * RING, one, 0)
            ring = 2 - stage // 3
            axis = order[ring]
            lead = order[1] if ring == 2 else None
            free = {order[1]: slice(None)} if ring == 2 else {}
            far, near, back = bufs[((2 - ring) * 4 + stream) * 3 + p]
            at = lambda s: place(p, stream, **free, **{axis: moved(me, axis, s)[axis]})
            if stage % 3 == 0:
                state[p, stream, ring, "far"] = links.push(held(at(2), u0, n), far, moved(me, axis, way))
                state[p, stream, ring, "back"] = links.push(held(at(-way), u0, n), back, moved(me, axis, -way))
            elif stage % 3 == 1:
                state[p, stream, ring, "far"].wait_recv()
                add(at(way), u0, n, far, lead)
                state[p, stream, ring, "near"] = links.push(held(at(way), u0, n), near, moved(me, axis, way))
            else:
                state[p, stream, ring, "back"].wait_recv()
                add(at(0), u0, n, back, lead)
                state[p, stream, ring, "near"].wait_recv()
                add(at(0), u0, n, near, lead)
                if ring == 1 and step != 0:
                    state[p, stream, "last"] = links.push(
                        held(place(p, stream), u0, n), bufs[24 + stream * 3 + p][0], moved(me, order[0], step)
                    )
    for stream in range(3):
        for p, (u0, n, order) in enumerate(ROW_PARTS):
            state[p, stream, "last"].wait_recv()
            add(me, u0, n, bufs[24 + stream * 3 + p][0], None)
    done = from_units(terms[me["x"], me["z"], me["c"], me["y"]], out.shape[0])
    out_v[...] = (mid[...].astype(f32) + done.astype(f32)).astype(bf16)
    write = pltpu.make_async_copy(out_v, out, local_sem)
    write.start()
    write.wait()
    links.finish()


def row_sum(slot, made, mid):
    rows, cols = mid.shape
    units = rows * cols // (UNIT[0] * UNIT[1])
    n = 12 + 3 * (4 * 6 + 3)
    bufs = []
    for ring in (2, 1):
        for stream in range(4):
            for _, count, _ in ROW_PARTS:
                bufs += [((RING,) if ring == 2 else ()) + (count,) + UNIT] * 3
    for stream in range(3):
        for _, count, _ in ROW_PARTS:
            bufs += [(count,) + UNIT]

    def kernel(slot, source, mid, out, terms, made, other, *rest):
        flat, rest = rest[: len(bufs)], rest[len(bufs) :]
        sets = [flat[3 * k : 3 * k + 3] for k in range(24)] + [flat[72 + k : 73 + k] for k in range(9)]
        row_sum_kernel(slot, source, mid, out, terms, made, other, sets, *rest)

    return pl.pallas_call(
        kernel,
        out_shape=jax.ShapeDtypeStruct((rows, cols), bf16),
        in_specs=[WHOLE, ANY, WHOLE],
        out_specs=ANY,
        scratch_shapes=[
            pltpu.VMEM((RING, RING, 2, RING, units) + UNIT, bf16),
            pltpu.VMEM(made.shape, bf16),
            pltpu.VMEM((RING, RING, RING, units) + UNIT, bf16),
        ]
        + [pltpu.VMEM(shape, bf16) for shape in bufs]
        + [
            pltpu.VMEM((rows, cols), bf16),
            pltpu.SemaphoreType.DMA((n,)),
            pltpu.SemaphoreType.DMA((n,)),
            pltpu.SemaphoreType.DMA,
            pltpu.SemaphoreType.DMA((RING,)),
        ],
        compiler_params=pltpu.CompilerParams(
            collective_id=3, has_side_effects=True, vmem_limit_bytes=58 << 20
        ),
        name="row_sum",
    )(slot, made, mid)


def attend_kernel(
    where, pages, queries, first, gathered, w_out, terms, cache, slot, gates,
    full, wo, zeros, attended, sems, page_sems,
):
    span = min(9, full.shape[0])
    block, start = where[0], where[1]
    slots = cache.shape[0]
    rows = queries.shape[0]
    grab = pltpu.make_async_copy(gathered, full, sems.at[0])
    grab.start()
    load = pltpu.make_async_copy(w_out, wo, sems.at[1])
    load.start()
    zeros[...] = jnp.zeros_like(zeros)

    def page_copy(n, page):
        return pltpu.make_async_copy(
            full.at[page // 8, pl.ds(pl.multiple_of(lax.rem(page, 8) * PAGE, PAGE), PAGE), :],
            cache.at[n],
            page_sems.at[n],
        )

    def empty_copy(n):
        return pltpu.make_async_copy(zeros, cache.at[n], page_sems.at[n])

    def send(n, carry):
        page = pages[n]

        @pl.when(page >= 0)
        def _():
            page_copy(n, page).start()

        @pl.when(page < 0)
        def _():
            empty_copy(n).start()

        return carry

    grab.wait()
    lax.fori_loop(0, slots, send, 0)
    width = span * rows
    held = full[pl.ds(start, span), :rows, :]
    keys = held[:, :, :HEAD_DIM].reshape(width, HEAD_DIM)
    values = held[:, :, HEAD_DIM:].reshape(width, HEAD_DIM)
    key_at = start * rows + lax.broadcasted_iota(jnp.int32, (rows, width), 1)
    query_at = block * rows + lax.broadcasted_iota(jnp.int32, (rows, width), 0)
    allowed = (key_at <= query_at) & (key_at >= first[...])
    for head in range(queries.shape[1] // HEAD_DIM):
        cols = pl.ds(head * HEAD_DIM, HEAD_DIM)
        scores = lax.dot_general(
            queries[:, cols], keys, (((1,), (1,)), ((), ())), preferred_element_type=f32
        ) * (HEAD_DIM**-0.5)
        scores = jnp.where(allowed, scores, masked_score)
        weights = jnp.where(allowed, jnp.exp(scores - jnp.max(scores, axis=1, keepdims=True)), 0.0)
        totals = jnp.sum(weights, axis=1, keepdims=True)
        mixed = jnp.dot(weights.astype(bf16), values, preferred_element_type=f32)
        attended[:, cols] = (mixed / totals).astype(bf16)
    load.wait()
    out_width = terms.shape[2]
    for half in range(2):
        cols = slice(2 * half * out_width, 2 * (half + 1) * out_width)
        part = jnp.dot(attended[...], wo[:, cols], preferred_element_type=f32).astype(bf16)
        terms[2 * half] = part[:, :out_width]
        terms[2 * half + 1] = part[:, out_width:]
    meta = full[:, rows : rows + 16, :]
    ids = meta[:, :TOP, :HEAD_DIM].astype(f32)
    weight = meta[:, 8 : 8 + TOP, :HEAD_DIM].astype(f32) + meta[:, 8 : 8 + TOP, HEAD_DIM:].astype(f32)
    blocks = meta.shape[0]
    earlier = lax.broadcasted_iota(jnp.int32, (rows, rows), 0) < lax.broadcasted_iota(jnp.int32, (rows, rows), 1)
    earlier = earlier.astype(f32).astype(bf16)
    odd = lax.rem(lax.broadcasted_iota(jnp.int32, (blocks, rows), 0), PAIR).astype(f32) * CAP
    n_exp = slot.shape[0]
    for e in range(n_exp):
        hits = ids == (block * n_exp + e).astype(f32)
        named = jnp.max(hits.astype(f32), axis=1)
        rank = jnp.dot(named.astype(bf16), earlier, preferred_element_type=f32)
        place = jnp.where(named > 0.0, rank + odd, -1.0)
        slot[e] = jnp.concatenate([place.reshape(blocks // PAIR, PAIR, rows)[:, b] for b in range(PAIR)], axis=1)
        share = jnp.sum(jnp.where(hits, weight, 0.0), axis=1)
        gates[e] = jnp.concatenate([share.reshape(blocks // PAIR, PAIR, rows)[:, b] for b in range(PAIR)], axis=1)

    def settle(n, carry):
        empty_copy(n).wait()
        return carry

    lax.fori_loop(0, slots, settle, 0)


def attend(block, pages, slots, queries, first, gathered, w_out, n_exp):
    blocks = gathered.shape[0]
    span = min(9, blocks)
    start = jnp.clip(block - 8, 0, blocks - span)
    width = gathered.shape[2]
    rows = queries.shape[0]
    terms = (RING, rows, w_out.shape[1] // RING)
    slot = (n_exp, blocks // PAIR, PAIR * rows)

    def whole(shape):
        return pl.BlockSpec(shape, lambda i, *_: (0,) * len(shape))

    return pl.pallas_call(
        attend_kernel,
        grid_spec=pltpu.PrefetchScalarGridSpec(
            num_scalar_prefetch=2,
            grid=(1,),
            in_specs=[whole(queries.shape), whole(first.shape), ANY, ANY],
            out_specs=(whole(terms), ANY, whole(slot), whole(slot)),
            scratch_shapes=[
                pltpu.VMEM(gathered.shape, bf16),
                pltpu.VMEM(w_out.shape, bf16),
                pltpu.VMEM((PAGE, width), bf16),
                pltpu.VMEM(queries.shape, bf16),
                pltpu.SemaphoreType.DMA((2,)),
                pltpu.SemaphoreType.DMA((slots,)),
            ],
        ),
        out_shape=(
            jax.ShapeDtypeStruct(terms, bf16),
            jax.ShapeDtypeStruct((slots, PAGE, width), bf16),
            jax.ShapeDtypeStruct(slot, f32),
            jax.ShapeDtypeStruct(slot, f32),
        ),
        compiler_params=pltpu.CompilerParams(vmem_limit_bytes=58 << 20),
        name="attend",
    )(jnp.stack([block, start]).astype(jnp.int32), pages, queries, first, gathered, w_out)


PAIR = 2


def expert_kernel(slot, gates, rows, w_gate, w_up, w_down, made, packed, scale, wgu, wd, sems, out_sems):
    step = pl.program_id(0)
    groups = 8
    tokens = groups * UNIT[0]
    tiles = rows.shape[4] // groups
    quarter = tiles * UNIT[1]
    pair_cap = PAIR * CAP
    n_exp, _, ff = w_gate.shape
    loads = [
        pltpu.make_async_copy(src, dst, sems.at[n])
        for n, (src, dst) in enumerate(
            ((w_gate, wgu.at[:, :, pl.ds(0, ff)]), (w_up, wgu.at[:, :, pl.ds(ff, ff)]), (w_down, wd))
        )
    ]

    @pl.when(step == 0)
    def _():
        for load in loads:
            load.start()

    row = lax.broadcasted_iota(jnp.int32, (pair_cap, PAIR * tokens), 0).astype(f32)
    for z in range(RING):
        span = pl.ds(pl.multiple_of((step * RING + z) * pair_cap, 16), pair_cap)
        same = [jnp.broadcast_to(slot[e, pl.ds(step * RING + z, 1), :], row.shape) == row for e in range(n_exp)]
        for e in range(n_exp):
            scale[e, span, :] = jnp.sum(
                jnp.where(same[e], gates[e, pl.ds(step * RING + z, 1), :], 0.0), axis=1, keepdims=True
            )
        pick = jnp.concatenate([m.astype(f32) for m in same], axis=0).astype(bf16)
        for h in range(2):
            parts = []
            for k in range(2):
                for j in range(tiles):
                    units = slice(j * groups, (j + 1) * groups)
                    parts.append(rows[0, z, :, 2 * h + k, units].reshape(PAIR * tokens, 128))
            got = jnp.dot(pick, jnp.concatenate(parts, axis=1), preferred_element_type=f32).astype(bf16)
            for e in range(n_exp):
                packed[e, span, 2 * h * quarter : 2 * (h + 1) * quarter] = got[e * pair_cap : (e + 1) * pair_cap]

    @pl.when(step == RING - 1)
    def _():
        for load in loads:
            load.wait()
        stores = []
        for e in range(n_exp):
            both = jnp.dot(packed[e], wgu[e], preferred_element_type=f32)
            gate_term, up_term = both[:, :ff], both[:, ff:]
            act = (gate_term / (1.0 + jnp.exp(-gate_term)) * up_term).astype(bf16)
            for h in range(2):
                cols = slice(2 * h * quarter, 2 * (h + 1) * quarter)
                down = jnp.dot(act, wd[e, :, cols], preferred_element_type=f32)
                packed[e, :, cols] = (down * scale[e]).astype(bf16)
            stores.append(pltpu.make_async_copy(packed.at[e], made.at[e], out_sems.at[e]))
            stores[e].start()
        for store in stores:
            store.wait()


def experts(slot, gates, rows, w_gate, w_up, w_down):
    n_exp, width, ff = w_gate.shape
    taken = (n_exp, RING * RING * PAIR * CAP)
    whole = pl.BlockSpec(slot.shape, lambda i: (0, 0, 0))
    some = pl.BlockSpec((1,) + rows.shape[1:], lambda i: (i,) + (0,) * (len(rows.shape) - 1))
    return pl.pallas_call(
        expert_kernel,
        grid=(RING,),
        in_specs=[whole, whole, some, ANY, ANY, ANY],
        out_specs=ANY,
        out_shape=jax.ShapeDtypeStruct(taken + (width,), bf16),
        scratch_shapes=[
            pltpu.VMEM(taken + (width,), bf16),
            pltpu.VMEM(taken + (1,), f32),
            pltpu.VMEM((n_exp, width, 2 * ff), bf16),
            pltpu.VMEM(w_down.shape, bf16),
            pltpu.SemaphoreType.DMA((3,)),
            pltpu.SemaphoreType.DMA((n_exp,)),
        ],
        compiler_params=pltpu.CompilerParams(vmem_limit_bytes=56 << 20),
        name="experts",
    )(slot, gates, rows, w_gate, w_up, w_down)


def local(
    hidden, gain_attn, w_query, w_key, w_value, w_out, gain_moe, expert_ids, expert_gates,
    w_gate, w_up, w_down, seg_lengths, slot_page,
):
    shard_count = lax.axis_size("seq")
    shard_index = lax.axis_index("seq")
    steps = np.arange(HEAD_DIM, dtype=np.float32) % (HEAD_DIM // 2)
    inverse = jnp.asarray(np.float32(rope_base) ** (np.float32(-2.0) * steps / np.float32(HEAD_DIM)))[None, :]
    gathered, queries, first = front(
        seg_lengths, hidden, gain_attn.reshape(-1, 128), inverse, expert_ids.T, expert_gates.T, w_query, w_key, w_value
    )
    gathered = gathered.reshape((shard_count,) + gathered.shape[3:])
    slot_count = slot_page.shape[0] // shard_count
    own_slots = lax.dynamic_slice_in_dim(slot_page, shard_index * slot_count, slot_count)
    terms, kv_cache, slot, gates = attend(
        shard_index, own_slots, slot_count, queries, first, gathered, w_out, w_gate.shape[0]
    )
    rows, mid = row_gather(terms, hidden, gain_moe.reshape(-1, 128))
    made = experts(slot, gates, rows, w_gate, w_up, w_down)
    return (row_sum(slot, made, mid), kv_cache)


def solution(mesh):
    placed = (
        P("seq", None),
        P(),
        P(None, "tp"),
        P(None, "tp"),
        P(None, "tp"),
        P("tp", None),
        P(),
        P("seq", None),
        P("seq", None),
        P("seq", None, "tp"),
        P("seq", None, "tp"),
        P("seq", "tp", None),
        P(),
        P(),
    )
    return jax.shard_map(
        local,
        mesh=mesh,
        in_specs=placed,
        out_specs=(P("seq", "tp"), P("seq", None, "tp")),
        check_vma=False,
    )
```

```python
import functools

import jax
import jax.numpy as jnp
import numpy as np
from jax import lax
from jax.experimental import pallas as pl
from jax.experimental.pallas import tpu as pltpu
from jax.sharding import PartitionSpec as P

HEAD_DIM = 128
TOP = 6
PAGE = 16
CAP = 24
RING = 4
MESH = pl.DeviceIdType.MESH
ANY = pl.BlockSpec(memory_space=pl.ANY)
WHOLE = pl.BlockSpec(memory_space=pltpu.VMEM)
epsilon = 1e-05
rope_base = 500000.0
masked_score = -1e30
bf16 = jnp.bfloat16
f32 = jnp.float32


def my_place():
    index = lax.axis_index("seq")
    return {
        "x": index // 8,
        "z": lax.rem(index // 2, RING),
        "c": lax.rem(index, 2),
        "y": lax.axis_index("tp"),
    }


def device_at(place):
    return ((place["x"] * RING + place["z"]) * 2 + place["c"], place["y"])


def moved(place, axis, step):
    size = 2 if axis == "c" else RING
    other = dict(place)
    other[axis] = lax.rem(place[axis] + step + size, size)
    return other


def enter(places):
    barrier = pltpu.get_barrier_semaphore()
    for place in places:
        pl.semaphore_signal(barrier, inc=1, device_id=device_at(place), device_id_type=MESH)
    pl.semaphore_wait(barrier, len(places))


class Links:
    def __init__(self, send_sem, recv_sem):
        self.send_sem, self.recv_sem, self.count = send_sem, recv_sem, 0
        self.started = []

    def push(self, src, dst, place):
        copy = pltpu.make_async_remote_copy(
            src_ref=src,
            dst_ref=dst,
            send_sem=self.send_sem.at[self.count],
            recv_sem=self.recv_sem.at[self.count],
            device_id=device_at(place),
            device_id_type=MESH,
        )
        self.count += 1
        copy.start()
        self.started.append(copy)
        return copy

    def finish(self):
        for copy in self.started:
            copy.wait_send()


def torus_gather(me, dims, parts, src, out, links, local_sem, beside):
    sibling = moved(me, "c", 1)

    def at(where, row0, rows):
        return out.at[tuple(where[d] for d in dims) + (pl.ds(row0, rows), slice(None))]

    own = {d: me[d] for d in dims}
    local = pltpu.make_async_copy(src, at(own, 0, src.shape[0]), local_sem)
    local.start()
    to_sibling = []
    for phase in range(len(parts[0][2])):
        if phase == 1:
            local.wait()
        live = []
        for row0, rows, order in parts:
            axis = order[phase]
            base = dict(own)
            for done in order[:phase]:
                base[done] = slice(None)
            whole = at(base, row0, rows)
            source = src.at[pl.ds(row0, rows), :] if phase == 0 else whole
            for step in (1, -1, 2):
                live.append((row0, rows, axis, base, step, links.push(source, whole, moved(me, axis, step))))
        if phase == 0:
            to_sibling.append(links.push(src, at(own, 0, src.shape[0]), sibling))
            beside()
        for row0, rows, axis, base, step, copy in live:
            copy.wait_recv()
            there = at({**base, axis: moved(me, axis, -step)[axis]}, row0, rows)
            to_sibling.append(links.push(there, there, sibling))
    for copy in to_sibling:
        copy.wait_recv()


def copies_of_gather(parts):
    return 1 + len(parts[0][2]) * len(parts) * 6


KV_PARTS = ((0, 80, ("x", "z")), (80, 64, ("z", "x")))
UNIT = (16, 128)
ROW_PARTS = (
    (0, 14, ("z", "y", "x")),
    (14, 13, ("y", "x", "z")),
    (27, 13, ("x", "z", "y")),
)
STREAMS = ((0, 1), (1, -1), (-1, 1), (2, -1))


def wave(stages):
    for stage in range(stages):
        for n in range(len(STREAMS)):
            yield stage, n


def to_units(values):
    rows, cols = values.shape
    return [
        values[:, j * 128 : (j + 1) * 128].reshape(rows // 16, 16, 128) for j in range(cols // 128)
    ]


def from_units(units, rows):
    group = rows // 16
    tiles = [units[j * group : (j + 1) * group].reshape(rows, 128) for j in range(units.shape[0] // group)]
    return jnp.concatenate(tiles, axis=1)


def stream_gather(me, src, out, links, local_sem):
    sibling = moved(me, "c", 1)

    def at(where, first, count):
        return out.at[where["x"], where["z"], where["c"], where["y"], pl.ds(first, count)]

    local = pltpu.make_async_copy(src, at(me, 0, src.shape[0]), local_sem)
    local.start()
    echo = []
    landed = {}
    for p, (u0, n, order) in enumerate(ROW_PARTS):
        piece = src.at[pl.ds(u0, n)]
        for step in (1, -1, 2):
            landed[p, step] = links.push(piece, at(me, u0, n), moved(me, order[0], step))
    state = {}

    def region(p, stream, ring, step):
        u0, n, order = ROW_PARTS[p]
        where = dict(me)
        where[order[0]] = moved(me, order[0], STREAMS[stream][0])[order[0]]
        if ring == 2:
            where[order[1]] = slice(None)
        where[order[ring]] = moved(me, order[ring], step)[order[ring]]
        return at(where, u0, n)

    def relay(ref):
        echo.append(links.push(ref, ref, sibling))

    for stage, stream in wave(6):
        step, way = STREAMS[stream]
        for p, (u0, n, order) in enumerate(ROW_PARTS):
            ring = 1 + stage // 3
            axis = order[ring]
            if stage % 3 == 0:
                if stage == 0:
                    if step == 0:
                        if p == 0:
                            local.wait()
                    else:
                        landed[p, -step if step != 2 else 2].wait_recv()
                else:
                    state[p, stream, 1, "far"].wait_recv()
                    whole = dict(me)
                    whole[order[0]] = moved(me, order[0], step)[order[0]]
                    whole[order[1]] = slice(None)
                    relay(at(whole, u0, n))
                own = region(p, stream, ring, 0)
                for w in (1, -1):
                    state[p, stream, ring, w] = links.push(own, own, moved(me, axis, w))
            elif stage % 3 == 1:
                state[p, stream, ring, way].wait_recv()
                near = region(p, stream, ring, -way)
                state[p, stream, ring, "far"] = links.push(near, near, moved(me, axis, way))
                state[p, stream, ring, -way].wait_recv()
                if ring == 2:
                    relay(near)
                    relay(region(p, stream, ring, way))
            elif ring == 2:
                state[p, stream, ring, "far"].wait_recv()
                relay(region(p, stream, ring, 2))
    for copy in echo:
        copy.wait_recv()


STREAM_COPIES = len(ROW_PARTS) * (3 + 4 * (3 + 4 + 3))


def turn(one, cosine, sine):
    return one * cosine + pltpu.roll(one, HEAD_DIM // 2, 1) * sine


def flat_gain(gain, first, count):
    return jnp.concatenate([gain[pl.ds(first + j, 1), :] for j in range(count)], axis=1)


def front_kernel(
    lengths, hidden, gain, inverse, expert_ids, expert_gates, w_query, w_key, w_value,
    gathered, queries, first, sent, wq, wk, wv, normed, send_sem, recv_sem, local_sem,
):
    me = my_place()
    loads = [
        pltpu.make_async_copy(src, dst, local_sem.at[1 + n])
        for n, (src, dst) in enumerate(((w_key, wk), (w_value, wv), (w_query, wq)))
    ]
    for load in loads:
        load.start()
    rows = hidden.shape[0]
    block = (me["x"] * RING + me["z"]) * 2 + me["c"]
    at = block * rows + lax.broadcasted_iota(jnp.int32, (rows, 1), 0)
    begin = jnp.zeros((rows, 1), jnp.int32)
    running = lengths[0]
    for n in range(1, lengths.shape[0]):
        begin = jnp.where(at >= running, running, begin)
        running = running + lengths[n]
    first[...] = begin
    angles = (at - begin).astype(f32) * inverse[...]
    cosine = jnp.cos(angles)
    lane = lax.broadcasted_iota(jnp.int32, angles.shape, 1)
    sine = jnp.where(lane < HEAD_DIM // 2, -jnp.sin(angles), jnp.sin(angles))
    wide = hidden[...].astype(f32)
    factor = lax.rsqrt(jnp.mean(wide * wide, axis=1, keepdims=True) + epsilon)
    normed[...] = (wide * factor * flat_gain(gain, 0, gain.shape[0])).astype(bf16)
    high = expert_gates[...].astype(bf16)
    low = (expert_gates[...] - high.astype(f32)).astype(bf16)
    to_at = lax.broadcasted_iota(jnp.int32, (16, TOP), 0)
    from_at = lax.broadcasted_iota(jnp.int32, (16, TOP), 1)
    top = (from_at == to_at).astype(f32).astype(bf16)
    below = (from_at + 8 == to_at).astype(f32).astype(bf16)

    def placed(where, values):
        return jnp.dot(where, values, preferred_element_type=f32)

    listed = placed(top, expert_ids[...].astype(f32).astype(bf16)) + placed(below, high)
    sent[rows : rows + 16, :HEAD_DIM] = listed.astype(bf16)
    sent[rows : rows + 16, HEAD_DIM:] = placed(below, low).astype(bf16)
    loads[0].wait()
    key = jnp.dot(normed[...], wk[...], preferred_element_type=f32)
    sent[:rows, :HEAD_DIM] = turn(key, cosine, sine).astype(bf16)
    loads[1].wait()
    sent[:rows, HEAD_DIM:] = jnp.dot(normed[...], wv[...], preferred_element_type=f32).astype(bf16)
    enter([moved(me, a, s) for a in ("x", "z") for s in (1, -1, 2)] + [moved(me, "c", 1)])
    links = Links(send_sem, recv_sem)

    def beside():
        loads[2].wait()
        raw = jnp.dot(normed[...], wq[...], preferred_element_type=f32)
        for head in range(raw.shape[1] // HEAD_DIM):
            cols = slice(head * HEAD_DIM, (head + 1) * HEAD_DIM)
            queries[:, cols] = turn(raw[:, cols], cosine, sine).astype(bf16)

    torus_gather(me, ("x", "z", "c"), KV_PARTS, sent, gathered, links, local_sem.at[0], beside)
    links.finish()


def front(lengths, hidden, gain, inverse, expert_ids, expert_gates, w_query, w_key, w_value):
    n = copies_of_gather(KV_PARTS)
    rows = hidden.shape[0]
    width = w_key.shape[1] + w_value.shape[1]
    return pl.pallas_call(
        front_kernel,
        out_shape=(
            jax.ShapeDtypeStruct((RING, RING, 2, rows + 16, width), bf16),
            jax.ShapeDtypeStruct((rows, w_query.shape[1]), bf16),
            jax.ShapeDtypeStruct((rows, 1), jnp.int32),
        ),
        in_specs=[pl.BlockSpec(memory_space=pltpu.SMEM)] + [WHOLE] * 5 + [ANY] * 3,
        out_specs=(ANY, WHOLE, WHOLE),
        scratch_shapes=[
            pltpu.VMEM((rows + 16, width), bf16),
            pltpu.VMEM(w_query.shape, bf16),
            pltpu.VMEM(w_key.shape, bf16),
            pltpu.VMEM(w_value.shape, bf16),
            pltpu.VMEM(hidden.shape, bf16),
            pltpu.SemaphoreType.DMA((n,)),
            pltpu.SemaphoreType.DMA((n,)),
            pltpu.SemaphoreType.DMA((4,)),
        ],
        compiler_params=pltpu.CompilerParams(
            collective_id=1, has_side_effects=True, vmem_limit_bytes=58 << 20
        ),
        name="front",
    )(lengths, hidden, gain, inverse, expert_ids, expert_gates, w_query, w_key, w_value)


def row_gather_kernel(
    terms, hidden, gain, out, mid, heard, squares, mid_v, row_v, send_sem, recv_sem, local_sem
):
    me = my_place()
    width = mid.shape[1]
    mine = pl.ds(pl.multiple_of(me["y"] * width, 128), width)
    peers = [moved(me, "y", s) for s in (1, 2, 3)]
    enter([moved(me, a, s) for a in ("x", "z") for s in (1, -1, 2)] + [moved(me, "c", 1)] + peers)
    links = Links(send_sem, recv_sem)
    sent = [
        links.push(terms.at[peer["y"]], heard.at[n], peer) for n, peer in enumerate(peers)
    ]
    total = terms[me["y"]].astype(f32)
    for n in range(3):
        sent[n].wait_recv()
        total = total + heard[n].astype(f32)
    mid_now = (hidden[:, mine].astype(f32) + total).astype(bf16)
    mid_v[...] = mid_now
    wide = mid_now.astype(f32)
    ours = jnp.sum(wide * wide, axis=1, keepdims=True)
    squares[3] = jnp.broadcast_to(ours, (ours.shape[0], 128)).T[:8]
    told = [links.push(squares.at[3], squares.at[n], peer) for n, peer in enumerate(peers)]
    whole = squares[3]
    for n in range(3):
        told[n].wait_recv()
        whole = whole + squares[n]
    whole = jnp.broadcast_to(whole[:1], (128, 128)).T[:, :1]
    factor = lax.rsqrt(whole * (1.0 / (RING * wide.shape[1])) + epsilon)
    ready = (wide * factor * flat_gain(gain, me["y"] * (width // 128), width // 128)).astype(bf16)
    for j, tile in enumerate(to_units(ready)):
        row_v[j * tile.shape[0] : (j + 1) * tile.shape[0]] = tile
    keep = pltpu.make_async_copy(mid_v, mid, local_sem.at[1])
    keep.start()
    stream_gather(me, row_v, out, links, local_sem.at[0])
    keep.wait()
    links.finish()


def row_gather(terms, hidden, gain):
    n = 6 + STREAM_COPIES
    rows, cols = terms.shape[1:]
    units = rows * cols // (UNIT[0] * UNIT[1])
    return pl.pallas_call(
        row_gather_kernel,
        out_shape=(
            jax.ShapeDtypeStruct((RING, RING, 2, RING, units) + UNIT, bf16),
            jax.ShapeDtypeStruct((rows, cols), bf16),
        ),
        in_specs=[WHOLE, WHOLE, WHOLE],
        out_specs=(ANY, ANY),
        scratch_shapes=[
            pltpu.VMEM((3, rows, cols), bf16),
            pltpu.VMEM((4, 8, rows), f32),
            pltpu.VMEM((rows, cols), bf16),
            pltpu.VMEM((units,) + UNIT, bf16),
            pltpu.SemaphoreType.DMA((n,)),
            pltpu.SemaphoreType.DMA((n,)),
            pltpu.SemaphoreType.DMA((2,)),
        ],
        compiler_params=pltpu.CompilerParams(
            collective_id=2, has_side_effects=True, vmem_limit_bytes=48 << 20
        ),
        name="row_gather",
    )(terms, hidden, gain)


SUM_DIMS = ("x", "z", "y")
SUM_STREAMS = ((2, 1), (1, -1), (-1, 1), (0, -1))


def row_sum_kernel(slot, source, mid, out, terms, made, other, bufs, out_v, send_sem, recv_sem, local_sem, in_sems):
    me = my_place()
    takes = []
    for x in range(RING):
        rows = pl.ds(x * RING * PAIR * CAP, RING * PAIR * CAP)
        takes.append(pltpu.make_async_copy(source.at[:, rows, :], made.at[:, rows, :], in_sems.at[x]))
        takes[x].start()
    sibling = moved(me, "c", 1)
    enter([moved(me, a, s) for a in ("x", "z", "y") for s in (1, -1, 2)] + [sibling])
    links = Links(send_sem, recv_sem)

    groups = 8
    tokens = groups * UNIT[0]
    tiles = terms.shape[4] // groups
    pair_cap = PAIR * CAP
    n_exp, _, width = made.shape

    def spread(x, z):
        chip = x * RING + z
        at = pl.multiple_of(chip * pair_cap, 16)
        row = lax.broadcasted_iota(jnp.int32, (pair_cap, PAIR * tokens), 0).astype(f32)
        same = [jnp.broadcast_to(slot[e, pl.ds(chip, 1), :], row.shape) == row for e in range(n_exp)]
        pick = jnp.concatenate([m.astype(f32) for m in same], axis=0).astype(bf16)
        for h in range(2):
            cols = slice(h * width // 2, (h + 1) * width // 2)
            rows = jnp.concatenate([made[e, pl.ds(at, pair_cap), cols] for e in range(n_exp)], axis=0)
            back = lax.dot_general(pick, rows, (((0,), (0,)), ((), ())), preferred_element_type=f32).astype(bf16)
            for k in range(2):
                for j in range(tiles):
                    n = k * tiles + j
                    terms[x, z, :, 2 * h + k, j * groups : (j + 1) * groups] = back[:, n * 128 : (n + 1) * 128].reshape(
                        PAIR, groups, *UNIT
                    )

    def one_chip(chip, carry):
        spread(chip // RING, chip % RING)
        return carry

    exchanged = []
    for x in range(RING):
        takes[x].wait()
        if x < RING - 1:
            lax.fori_loop(x * RING, (x + 1) * RING, one_chip, 0)
            exchanged.append(links.push(terms.at[x, :, sibling["c"]], other.at[x], sibling))
            continue
        for z in range(RING):
            one_chip(x * RING + z, 0)
            exchanged.append(links.push(terms.at[x, z, sibling["c"]], other.at[x, z], sibling))

    def held(where, u0, n):
        return terms.at[where["x"], where["z"], me["c"], where["y"], pl.ds(u0, n)]

    def place(p, stream, **free):
        order = ROW_PARTS[p][2]
        where = dict(me)
        where[order[0]] = moved(me, order[0], SUM_STREAMS[stream][0])[order[0]]
        where.update(free)
        return where

    def add(where, u0, n, buf, lead):
        span = pl.ds(u0, n)
        if lead is None:
            index = (where["x"], where["z"], me["c"], where["y"], span)
            terms[index] = terms[index] + buf[...]
            return

        def one(k, carry):
            spot = {**where, lead: k}
            index = (spot["x"], spot["z"], me["c"], spot["y"], span)
            terms[index] = terms[index] + buf[k]
            return carry

        lax.fori_loop(0, RING, one, 0)

    state = {}
    for stage, stream in wave(6):
        step, way = SUM_STREAMS[stream]
        for p, (u0, n, order) in enumerate(ROW_PARTS):
            if stage == 0:
                if stream == 0 and p == 0:
                    for push in exchanged:
                        push.wait_recv()
                where = place(p, stream)
                span = pl.ds(u0, n)

                def one(k, carry, where=where, span=span, order=order):
                    spot = {order[1]: k // RING, order[2]: lax.rem(k, RING)}
                    x, z, y = (spot.get(d, where[d]) for d in SUM_DIMS)
                    terms[x, z, me["c"], y, span] = terms[x, z, me["c"], y, span] + other[x, z, y, span]
                    return carry

                lax.fori_loop(0, RING * RING, one, 0)
            ring = 2 - stage // 3
            axis = order[ring]
            lead = order[1] if ring == 2 else None
            free = {order[1]: slice(None)} if ring == 2 else {}
            far, near, back = bufs[((2 - ring) * 4 + stream) * 3 + p]
            at = lambda s: place(p, stream, **free, **{axis: moved(me, axis, s)[axis]})
            if stage % 3 == 0:
                state[p, stream, ring, "far"] = links.push(held(at(2), u0, n), far, moved(me, axis, way))
                state[p, stream, ring, "back"] = links.push(held(at(-way), u0, n), back, moved(me, axis, -way))
            elif stage % 3 == 1:
                state[p, stream, ring, "far"].wait_recv()
                add(at(way), u0, n, far, lead)
                state[p, stream, ring, "near"] = links.push(held(at(way), u0, n), near, moved(me, axis, way))
            else:
                state[p, stream, ring, "back"].wait_recv()
                add(at(0), u0, n, back, lead)
                state[p, stream, ring, "near"].wait_recv()
                add(at(0), u0, n, near, lead)
                if ring == 1 and step != 0:
                    state[p, stream, "last"] = links.push(
                        held(place(p, stream), u0, n), bufs[24 + stream * 3 + p][0], moved(me, order[0], step)
                    )
    for stream in range(3):
        for p, (u0, n, order) in enumerate(ROW_PARTS):
            state[p, stream, "last"].wait_recv()
            add(me, u0, n, bufs[24 + stream * 3 + p][0], None)
    done = from_units(terms[me["x"], me["z"], me["c"], me["y"]], out.shape[0])
    out_v[...] = (mid[...].astype(f32) + done.astype(f32)).astype(bf16)
    write = pltpu.make_async_copy(out_v, out, local_sem)
    write.start()
    write.wait()
    links.finish()


def row_sum(slot, made, mid):
    rows, cols = mid.shape
    units = rows * cols // (UNIT[0] * UNIT[1])
    n = 2 * RING - 1 + 3 * (4 * 6 + 3)
    bufs = []
    for ring in (2, 1):
        for stream in range(4):
            for _, count, _ in ROW_PARTS:
                bufs += [((RING,) if ring == 2 else ()) + (count,) + UNIT] * 3
    for stream in range(3):
        for _, count, _ in ROW_PARTS:
            bufs += [(count,) + UNIT]

    def kernel(slot, source, mid, out, terms, made, other, *rest):
        flat, rest = rest[: len(bufs)], rest[len(bufs) :]
        sets = [flat[3 * k : 3 * k + 3] for k in range(24)] + [flat[72 + k : 73 + k] for k in range(9)]
        row_sum_kernel(slot, source, mid, out, terms, made, other, sets, *rest)

    return pl.pallas_call(
        kernel,
        out_shape=jax.ShapeDtypeStruct((rows, cols), bf16),
        in_specs=[WHOLE, ANY, WHOLE],
        out_specs=ANY,
        scratch_shapes=[
            pltpu.VMEM((RING, RING, 2, RING, units) + UNIT, bf16),
            pltpu.VMEM(made.shape, bf16),
            pltpu.VMEM((RING, RING, RING, units) + UNIT, bf16),
        ]
        + [pltpu.VMEM(shape, bf16) for shape in bufs]
        + [
            pltpu.VMEM((rows, cols), bf16),
            pltpu.SemaphoreType.DMA((n,)),
            pltpu.SemaphoreType.DMA((n,)),
            pltpu.SemaphoreType.DMA,
            pltpu.SemaphoreType.DMA((RING,)),
        ],
        compiler_params=pltpu.CompilerParams(
            collective_id=3, has_side_effects=True, vmem_limit_bytes=58 << 20
        ),
        name="row_sum",
    )(slot, made, mid)


def attend_kernel(
    where, pages, queries, first, gathered, w_out, terms, cache, slot, gates,
    full, wo, zeros, attended, sems, page_sems,
):
    span = min(9, full.shape[0])
    block, start = where[0], where[1]
    slots = cache.shape[0]
    rows = queries.shape[0]
    grab = pltpu.make_async_copy(gathered, full, sems.at[0])
    grab.start()
    load = pltpu.make_async_copy(w_out, wo, sems.at[1])
    load.start()
    zeros[...] = jnp.zeros_like(zeros)

    def page_copy(n, page):
        return pltpu.make_async_copy(
            full.at[page // 8, pl.ds(pl.multiple_of(lax.rem(page, 8) * PAGE, PAGE), PAGE), :],
            cache.at[n],
            page_sems.at[n],
        )

    def empty_copy(n):
        return pltpu.make_async_copy(zeros, cache.at[n], page_sems.at[n])

    def send(n, carry):
        page = pages[n]

        @pl.when(page >= 0)
        def _():
            page_copy(n, page).start()

        @pl.when(page < 0)
        def _():
            empty_copy(n).start()

        return carry

    grab.wait()
    lax.fori_loop(0, slots, send, 0)
    width = span * rows
    held = full[pl.ds(start, span), :rows, :]
    keys = held[:, :, :HEAD_DIM].reshape(width, HEAD_DIM)
    values = held[:, :, HEAD_DIM:].reshape(width, HEAD_DIM)
    key_at = start * rows + lax.broadcasted_iota(jnp.int32, (rows, width), 1)
    query_at = block * rows + lax.broadcasted_iota(jnp.int32, (rows, width), 0)
    allowed = (key_at <= query_at) & (key_at >= first[...])
    for head in range(queries.shape[1] // HEAD_DIM):
        cols = pl.ds(head * HEAD_DIM, HEAD_DIM)
        scores = lax.dot_general(
            queries[:, cols], keys, (((1,), (1,)), ((), ())), preferred_element_type=f32
        ) * (HEAD_DIM**-0.5)
        scores = jnp.where(allowed, scores, masked_score)
        weights = jnp.where(allowed, jnp.exp(scores - jnp.max(scores, axis=1, keepdims=True)), 0.0)
        totals = jnp.sum(weights, axis=1, keepdims=True)
        mixed = jnp.dot(weights.astype(bf16), values, preferred_element_type=f32)
        attended[:, cols] = (mixed / totals).astype(bf16)
    load.wait()
    out_width = terms.shape[2]
    for half in range(2):
        cols = slice(2 * half * out_width, 2 * (half + 1) * out_width)
        part = jnp.dot(attended[...], wo[:, cols], preferred_element_type=f32).astype(bf16)
        terms[2 * half] = part[:, :out_width]
        terms[2 * half + 1] = part[:, out_width:]
    meta = full[:, rows : rows + 16, :]
    ids = meta[:, :TOP, :HEAD_DIM].astype(f32)
    weight = meta[:, 8 : 8 + TOP, :HEAD_DIM].astype(f32) + meta[:, 8 : 8 + TOP, HEAD_DIM:].astype(f32)
    blocks = meta.shape[0]
    earlier = lax.broadcasted_iota(jnp.int32, (rows, rows), 0) < lax.broadcasted_iota(jnp.int32, (rows, rows), 1)
    earlier = earlier.astype(f32).astype(bf16)
    odd = lax.rem(lax.broadcasted_iota(jnp.int32, (blocks, rows), 0), PAIR).astype(f32) * CAP
    n_exp = slot.shape[0]
    for e in range(n_exp):
        hits = ids == (block * n_exp + e).astype(f32)
        named = jnp.max(hits.astype(f32), axis=1)
        rank = jnp.dot(named.astype(bf16), earlier, preferred_element_type=f32)
        place = jnp.where(named > 0.0, rank + odd, -1.0)
        slot[e] = jnp.concatenate([place.reshape(blocks // PAIR, PAIR, rows)[:, b] for b in range(PAIR)], axis=1)
        share = jnp.sum(jnp.where(hits, weight, 0.0), axis=1)
        gates[e] = jnp.concatenate([share.reshape(blocks // PAIR, PAIR, rows)[:, b] for b in range(PAIR)], axis=1)

    def settle(n, carry):
        empty_copy(n).wait()
        return carry

    lax.fori_loop(0, slots, settle, 0)


def attend(block, pages, slots, queries, first, gathered, w_out, n_exp):
    blocks = gathered.shape[0]
    span = min(9, blocks)
    start = jnp.clip(block - 8, 0, blocks - span)
    width = gathered.shape[2]
    rows = queries.shape[0]
    terms = (RING, rows, w_out.shape[1] // RING)
    slot = (n_exp, blocks // PAIR, PAIR * rows)

    def whole(shape):
        return pl.BlockSpec(shape, lambda i, *_: (0,) * len(shape))

    return pl.pallas_call(
        attend_kernel,
        grid_spec=pltpu.PrefetchScalarGridSpec(
            num_scalar_prefetch=2,
            grid=(1,),
            in_specs=[whole(queries.shape), whole(first.shape), ANY, ANY],
            out_specs=(whole(terms), ANY, whole(slot), whole(slot)),
            scratch_shapes=[
                pltpu.VMEM(gathered.shape, bf16),
                pltpu.VMEM(w_out.shape, bf16),
                pltpu.VMEM((PAGE, width), bf16),
                pltpu.VMEM(queries.shape, bf16),
                pltpu.SemaphoreType.DMA((2,)),
                pltpu.SemaphoreType.DMA((slots,)),
            ],
        ),
        out_shape=(
            jax.ShapeDtypeStruct(terms, bf16),
            jax.ShapeDtypeStruct((slots, PAGE, width), bf16),
            jax.ShapeDtypeStruct(slot, f32),
            jax.ShapeDtypeStruct(slot, f32),
        ),
        compiler_params=pltpu.CompilerParams(vmem_limit_bytes=58 << 20),
        name="attend",
    )(jnp.stack([block, start]).astype(jnp.int32), pages, queries, first, gathered, w_out)


PAIR = 2


def expert_kernel(slot, gates, rows, w_gate, w_up, w_down, made, packed, scale, wgu, wd, sems, out_sems):
    step = pl.program_id(0)
    groups = 8
    tokens = groups * UNIT[0]
    tiles = rows.shape[4] // groups
    quarter = tiles * UNIT[1]
    pair_cap = PAIR * CAP
    n_exp, _, ff = w_gate.shape
    loads = [
        pltpu.make_async_copy(src, dst, sems.at[n])
        for n, (src, dst) in enumerate(
            ((w_gate, wgu.at[:, :, pl.ds(0, ff)]), (w_up, wgu.at[:, :, pl.ds(ff, ff)]), (w_down, wd))
        )
    ]

    @pl.when(step == 0)
    def _():
        for load in loads:
            load.start()

    row = lax.broadcasted_iota(jnp.int32, (pair_cap, PAIR * tokens), 0).astype(f32)
    for z in range(RING):
        span = pl.ds(pl.multiple_of((step * RING + z) * pair_cap, 16), pair_cap)
        same = [jnp.broadcast_to(slot[e, pl.ds(step * RING + z, 1), :], row.shape) == row for e in range(n_exp)]
        for e in range(n_exp):
            scale[e, span, :] = jnp.sum(
                jnp.where(same[e], gates[e, pl.ds(step * RING + z, 1), :], 0.0), axis=1, keepdims=True
            )
        pick = jnp.concatenate([m.astype(f32) for m in same], axis=0).astype(bf16)
        for h in range(2):
            parts = []
            for k in range(2):
                for j in range(tiles):
                    units = slice(j * groups, (j + 1) * groups)
                    parts.append(rows[0, z, :, 2 * h + k, units].reshape(PAIR * tokens, 128))
            got = jnp.dot(pick, jnp.concatenate(parts, axis=1), preferred_element_type=f32).astype(bf16)
            for e in range(n_exp):
                packed[e, span, 2 * h * quarter : 2 * (h + 1) * quarter] = got[e * pair_cap : (e + 1) * pair_cap]

    @pl.when(step == RING - 1)
    def _():
        for load in loads:
            load.wait()
        stores = []
        for e in range(n_exp):
            both = jnp.dot(packed[e], wgu[e], preferred_element_type=f32)
            gate_term, up_term = both[:, :ff], both[:, ff:]
            act = (gate_term / (1.0 + jnp.exp(-gate_term)) * up_term).astype(bf16)
            for h in range(2):
                cols = slice(2 * h * quarter, 2 * (h + 1) * quarter)
                down = jnp.dot(act, wd[e, :, cols], preferred_element_type=f32)
                packed[e, :, cols] = (down * scale[e]).astype(bf16)
            stores.append(pltpu.make_async_copy(packed.at[e], made.at[e], out_sems.at[e]))
            stores[e].start()
        for store in stores:
            store.wait()


def experts(slot, gates, rows, w_gate, w_up, w_down):
    n_exp, width, ff = w_gate.shape
    taken = (n_exp, RING * RING * PAIR * CAP)
    whole = pl.BlockSpec(slot.shape, lambda i: (0, 0, 0))
    some = pl.BlockSpec((1,) + rows.shape[1:], lambda i: (i,) + (0,) * (len(rows.shape) - 1))
    return pl.pallas_call(
        expert_kernel,
        grid=(RING,),
        in_specs=[whole, whole, some, ANY, ANY, ANY],
        out_specs=ANY,
        out_shape=jax.ShapeDtypeStruct(taken + (width,), bf16),
        scratch_shapes=[
            pltpu.VMEM(taken + (width,), bf16),
            pltpu.VMEM(taken + (1,), f32),
            pltpu.VMEM((n_exp, width, 2 * ff), bf16),
            pltpu.VMEM(w_down.shape, bf16),
            pltpu.SemaphoreType.DMA((3,)),
            pltpu.SemaphoreType.DMA((n_exp,)),
        ],
        compiler_params=pltpu.CompilerParams(vmem_limit_bytes=56 << 20),
        name="experts",
    )(slot, gates, rows, w_gate, w_up, w_down)


def local(
    hidden, gain_attn, w_query, w_key, w_value, w_out, gain_moe, expert_ids, expert_gates,
    w_gate, w_up, w_down, seg_lengths, slot_page,
):
    shard_count = lax.axis_size("seq")
    shard_index = lax.axis_index("seq")
    steps = np.arange(HEAD_DIM, dtype=np.float32) % (HEAD_DIM // 2)
    inverse = jnp.asarray(np.float32(rope_base) ** (np.float32(-2.0) * steps / np.float32(HEAD_DIM)))[None, :]
    gathered, queries, first = front(
        seg_lengths, hidden, gain_attn.reshape(-1, 128), inverse, expert_ids.T, expert_gates.T, w_query, w_key, w_value
    )
    gathered = gathered.reshape((shard_count,) + gathered.shape[3:])
    slot_count = slot_page.shape[0] // shard_count
    own_slots = lax.dynamic_slice_in_dim(slot_page, shard_index * slot_count, slot_count)
    terms, kv_cache, slot, gates = attend(
        shard_index, own_slots, slot_count, queries, first, gathered, w_out, w_gate.shape[0]
    )
    rows, mid = row_gather(terms, hidden, gain_moe.reshape(-1, 128))
    made = experts(slot, gates, rows, w_gate, w_up, w_down)
    return (row_sum(slot, made, mid), kv_cache)


def solution(mesh):
    placed = (
        P("seq", None),
        P(),
        P(None, "tp"),
        P(None, "tp"),
        P(None, "tp"),
        P("tp", None),
        P(),
        P("seq", None),
        P("seq", None),
        P("seq", None, "tp"),
        P("seq", None, "tp"),
        P("seq", "tp", None),
        P(),
        P(),
    )
    return jax.shard_map(
        local,
        mesh=mesh,
        in_specs=placed,
        out_specs=(P("seq", "tp"), P("seq", None, "tp")),
        check_vma=False,
    )
```
